32 devices in a mesh: row: 4 (over y, x), col: 8 (over z, core).
Axes of the slice: x: 2, y: 2, z: 4, core: 2. Of those that a mesh axis runs over, the one named last changes fastest.
Arguments:
- wavefield: bfloat16 [2, 1, 8192, 8192], P(None, None, 'row', 'col'), as said below
- panel_order: int32 [16], replicated, may hold values from 0 to 15, each once
- filter_taps: float32 [11, 8192], P(None, 'col'), may hold values from -4 to 4
Outputs:
- primaries: bfloat16 [2, 1, 8192, 8192], P(None, None, 'row', 'col')
The draws below stay inside these ranges and needn't reach their ends.
Inputs may be any that keep to these rules, and one draw needn't show every extreme that they name: Reciprocity: wavefield[c, f, s, r] = wavefield[c, f, r, s] for every part, frequency, shot and receiver.
All inputs are finite; a program needn't handle non-finite values.
Results may differ from the reference program's by a relative error of at most 0.00045.
Values may be sent and summed in bfloat16 or wider, within the bound.
A program may use at most 128 MiB of HBM per device.

```python
import math
import jax
import jax.numpy as jnp
from jax import lax

SIDE = 8192
PANEL = 512
STEPS = 3
FREQ = 1
TAPS = 11
FIRST_FREQUENCY = 8
NT = 1024
NPANEL = 16


def draw_wavefield(key, part):
    first, second, third = jax.random.split(jax.random.fold_in(key, 17), 3)
    profile_key, phase_key = jax.random.split(third)
    position = jnp.arange(SIDE, dtype=jnp.float32) / SIDE
    jitter = jax.random.uniform(second, (SIDE,), jnp.float32)
    profile = jnp.clip(jax.random.normal(profile_key, (FREQ, SIDE), jnp.float32), -2.5, 2.5)
    angle = jax.random.uniform(phase_key, (FREQ,), jnp.float32, -3.14159265, 3.14159265)
    amplitude = 0.35 * jnp.stack([jnp.cos(angle), jnp.sin(angle)])
    base = jnp.clip(jax.random.normal(first, (2, FREQ, SIDE, SIDE), jnp.float32), -4.0, 4.0)
    weights = 10.0 ** (0.5 * position + 0.5 * jitter - 0.5)
    mirrored = (base + jnp.swapaxes(base, 2, 3)) * 0.70710678
    coherent = amplitude[:, :, None, None] * profile[None, :, :, None] * profile[None, :, None, :]
    mirrored = mirrored + coherent
    return (mirrored * weights[:, None] * weights[None, :]).astype(jnp.bfloat16)


def steps_of(rng, extent, cuts, smallest, largest):
    def one(axis_at, parts):
        heights = jax.random.uniform(jax.random.fold_in(jax.random.fold_in(rng, 6), axis_at), (parts,), jnp.float32, smallest / len(cuts), largest / len(cuts))
        return jnp.repeat(jnp.exp(heights), extent[axis_at] // parts).reshape((-1,) + (1,) * (len(extent) - axis_at - 1))

    level = one(*cuts[0])
    for cut in cuts[1:]:
        level = level * one(*cut)
    return level


def centred(rng, extent, spread, limit, shards=(), kind=jnp.bfloat16):
    values = spread * jax.random.normal(rng, extent, jnp.float32)
    if shards:
        values = values * steps_of(rng, extent, shards, -0.22, 0.18)
    return jnp.clip(values, -limit, limit).astype(kind)


def setup_inputs(seed: int = 0) -> dict:
    arg_keys = jax.random.split(jax.random.key(seed), 4)
    return {
        "wavefield": draw_wavefield(jax.random.fold_in(arg_keys[3], 71), 0),
        "panel_order": jax.random.permutation(arg_keys[1], NPANEL).astype(jnp.int32),
        "filter_taps": centred(arg_keys[2], (TAPS, SIDE), 0.3, 4.0, ((1, 8),), jnp.float32),
    }


def frequency_spectrum(filter_taps):
    lags = jnp.arange(TAPS, dtype=jnp.float32)
    omega = 2.0 * math.pi * (FIRST_FREQUENCY + jnp.arange(FREQ, dtype=jnp.float32)) / NT
    phase = omega[:, None] * lags[None, :]
    real_part = jnp.dot(jnp.cos(phase), filter_taps, precision=lax.Precision.HIGHEST)
    imag_part = -jnp.dot(jnp.sin(phase), filter_taps, precision=lax.Precision.HIGHEST)
    return (real_part, imag_part)

def reference(wavefield, panel_order, filter_taps):
    picks = (panel_order[:STEPS, None] * PANEL + jnp.arange(PANEL, dtype=jnp.int32)[None, :]).reshape(-1).astype(jnp.int32)
    spec_re, spectrum_imaginary = frequency_spectrum(filter_taps)
    factor = 1.0 / math.sqrt(STEPS * PANEL)
    count = 2.0 * SIDE * SIDE

    def one_slice(index):
        field = wavefield[:, index]
        upper = field[:, :, picks]
        lower = field[:, picks, :]
        left_factor = jnp.concatenate([upper[0], upper[1]], axis=1)
        right_factor = jnp.concatenate([jnp.concatenate([lower[0], lower[1]], axis=1), jnp.concatenate([-lower[1], lower[0]], axis=1)], axis=0)
        product = jnp.dot(left_factor, right_factor, preferred_element_type=jnp.float32) * factor
        mult_re = product[:, :SIDE]
        mult_im = product[:, SIDE:]
        energy_data = jnp.sum(jnp.square(field.astype(jnp.float32))) / count
        energy_mult = (jnp.sum(mult_re * mult_re) + jnp.sum(mult_im * mult_im)) / count
        gain = jnp.sqrt((energy_data + 1e-05) / (energy_mult + 1e-05))
        a_re = spec_re[index][None, :]
        a_im = spectrum_imaginary[index][None, :]
        sub_re = gain * (a_re * mult_re - a_im * mult_im)
        subtracted_imaginary = gain * (a_re * mult_im + a_im * mult_re)
        return jnp.stack([field[0].astype(jnp.float32) - sub_re, field[1].astype(jnp.float32) - subtracted_imaginary]).astype(jnp.bfloat16)
    result = lax.map(one_slice, jnp.arange(FREQ, dtype=jnp.int32))
    return jnp.swapaxes(result, 0, 1)
```

```python
import functools
import math

import jax
import jax.numpy as jnp
from jax import lax
from jax.experimental import pallas as pl
from jax.experimental.pallas import tpu as pltpu
from jax.sharding import PartitionSpec as P

SIDE = 8192
PANEL = 512
STEPS = 3
TAPS = 11
FIRST_FREQUENCY = 8
NT = 1024
MESH = pl.DeviceIdType.MESH

CHUNK = 64
NCHUNK = STEPS * PANEL // CHUNK
GROUP = 256 // CHUNK
NGROUP = NCHUNK // GROUP
TILE = 256
HOP = 1
LAG = 5 * HOP
AHEAD = 2
STRIP = 64


def spread(block, axis, holder):
    block = jnp.where(lax.axis_index(axis) == holder, block, jnp.zeros_like(block))
    return lax.psum(block, axis)


def frequency_spectrum(filter_taps, freq_count):
    lags = jnp.arange(TAPS, dtype=jnp.float32)
    omega = 2.0 * math.pi * (FIRST_FREQUENCY + jnp.arange(freq_count, dtype=jnp.float32)) / NT
    phase = omega[:, None] * lags[None, :]
    real_part = jnp.dot(jnp.cos(phase), filter_taps, precision=lax.Precision.HIGHEST)
    imag_part = -jnp.dot(jnp.sin(phase), filter_taps, precision=lax.Precision.HIGHEST)
    return (real_part, imag_part)


def local(wavefield, panel_order, filter_taps):
    freq_count = wavefield.shape[1]
    shot_block = wavefield.shape[2]
    recv_block = wavefield.shape[3]
    own_row_index = lax.axis_index("row")
    factor = 1.0 / math.sqrt(STEPS * PANEL)
    count = 2.0 * SIDE * SIDE
    local_data = jnp.sum(jnp.square(wavefield.astype(jnp.float32)), axis=(0, 2, 3))
    energy_data = lax.psum(local_data, ("row", "col"))
    totals = jnp.zeros((freq_count, shot_block, 2 * recv_block), jnp.float32)
    for panel_advance in range(STEPS):
        first_point = panel_order[panel_advance] * PANEL
        row_width = min(PANEL, shot_block)
        owner_turn = 0
        start = first_point + owner_turn * row_width
        piece = lax.dynamic_slice_in_dim(wavefield, start % shot_block, row_width, 2)
        row_pieces = spread(piece, "row", start // shot_block)
        col_pieces = []
        mirror_width = min(shot_block, recv_block)
        for owner_turn in range(max(1, shot_block // recv_block)):
            start = own_row_index * shot_block + owner_turn * mirror_width
            piece = row_pieces
            col_pieces.append(spread(piece, "col", start // recv_block))
        upper = jnp.swapaxes(jnp.concatenate(col_pieces, axis=3), 2, 3)
        left_factor = jnp.concatenate([upper[0], upper[1]], axis=2)
        right_factor = jnp.concatenate(
            [
                jnp.concatenate([row_pieces[0], row_pieces[1]], axis=2),
                jnp.concatenate([-row_pieces[1], row_pieces[0]], axis=2),
            ],
            axis=1,
        )
        totals = totals + jnp.einsum(
            "yga,yah->ygh", left_factor, right_factor, preferred_element_type=jnp.float32
        )
    mult_re = totals[:, :, :recv_block] * factor
    mult_im = totals[:, :, recv_block:] * factor
    local_mult = jnp.sum(mult_re * mult_re, axis=(1, 2)) + jnp.sum(mult_im * mult_im, axis=(1, 2))
    energy_mult = lax.psum(local_mult, ("row", "col"))
    gain = jnp.sqrt((energy_data / count + 1e-05) / (energy_mult / count + 1e-05))[:, None, None]
    spec_re, spectrum_imaginary = frequency_spectrum(filter_taps, freq_count)
    a_re = spec_re[:, None, :]
    a_im = spectrum_imaginary[:, None, :]
    sub_re = gain * (a_re * mult_re - a_im * mult_im)
    subtracted_imaginary = gain * (a_re * mult_im + a_im * mult_re)
    result = jnp.stack(
        [
            wavefield[0].astype(jnp.float32) - sub_re,
            wavefield[1].astype(jnp.float32) - subtracted_imaginary,
        ]
    )
    return result.astype(jnp.bfloat16)


def predict_kernel(variant, piece0, piece1, piece2, field, mult, gain,
                   own, first, second, left, acc, right, energy, strip, part_sums, row_sums, col_sums,
                   xs, xr, ys, yr, us, ds, zr, ps, pr, own_sem, out_sem, strip_sem,
                   rs, rr, cs, cr):
    panels = (piece0, piece1, piece2)
    per_panel = PANEL // CHUNK
    count = 2.0 * SIDE * SIDE
    factor = 1.0 / math.sqrt(STEPS * PANEL)
    row = lax.axis_index("row")
    col = lax.axis_index("col")
    z = col // 2
    core = col % 2
    along_x = row + 1 - 2 * (row % 2)
    along_y = (row + 2) % 4
    partner = col + 1 - 2 * core
    width = first.shape[3]
    above = z - row
    far = jnp.abs(above)

    loads = [
        pltpu.make_async_copy(panels[t], own.at[pl.ds(t * per_panel, per_panel)], own_sem.at[t])
        for t in range(STEPS)
    ]
    for load in loads:
        load.start()

    def strip_copy(s):
        return pltpu.make_async_copy(
            field.at[:, pl.ds(pl.multiple_of(s * STRIP, STRIP), STRIP), :],
            strip.at[s % 2], strip_sem.at[s % 2])

    nstrip = field.shape[1] // STRIP
    strip_copy(0).start()
    energy[...] = jnp.zeros_like(energy) + (0.0 * variant)
    barrier = pltpu.get_barrier_semaphore()
    for j in range(1, 4):
        pl.semaphore_signal(barrier, inc=1, device_id=((row + j) % 4, col), device_id_type=MESH)
    for j in range(1, 8):
        pl.semaphore_signal(barrier, inc=1, device_id=(row, (col + j) % 8), device_id_type=MESH)
    pl.semaphore_wait(barrier, 10)

    def x_copy(t, k):
        to = along_x + (k % 2) * (along_y - along_x)
        return pltpu.make_async_remote_copy(
            src_ref=panels[t].at[k - t * per_panel], dst_ref=first.at[k], send_sem=xs.at[k],
            recv_sem=xr.at[k], device_id=(to, col), device_id_type=MESH)

    def x_start(k):
        for t in range(STEPS):
            @pl.when(jnp.logical_and(k >= t * per_panel, k < (t + 1) * per_panel))
            def _():
                x_copy(t, k).start()

    def y_copy(k):
        to = along_y + (k % 2) * (along_x - along_y)
        return pltpu.make_async_remote_copy(
            src_ref=first.at[k], dst_ref=second.at[k], send_sem=ys.at[k], recv_sem=yr.at[k],
            device_id=(to, col), device_id_type=MESH)

    def z_copy(src, k, to, sem):
        return pltpu.make_async_remote_copy(
            src_ref=src, dst_ref=left.at[core, k], send_sem=sem.at[k], recv_sem=zr.at[k],
            device_id=(row, to), device_id_type=MESH)

    def p_copy(src, k):
        return pltpu.make_async_remote_copy(
            src_ref=src, dst_ref=left.at[core, k], send_sem=ps.at[k], recv_sem=pr.at[k],
            device_id=(row, partner), device_id_type=MESH)

    go_up = jnp.logical_and(above >= 0, z < 3)
    go_down = jnp.logical_and(above <= 0, z > 0)

    def pass_on(src, k):
        @pl.when(go_up)
        def _():
            z_copy(src, k, col + 2, us).start()

        @pl.when(go_down)
        def _():
            z_copy(src, k, col - 2, ds).start()

        p_copy(src, k).start()

    @pl.loop(0, AHEAD)
    def _(k):
        x_start(k)

    for load in loads:
        load.wait()

    def out_copy(part, at):
        return pltpu.make_async_copy(
            acc.at[part, pl.ds(at, TILE), :], mult.at[part, pl.ds(at, TILE), :], out_sem.at[0])

    @pl.loop(0, NCHUNK + LAG + GROUP - 1)
    def _(s):
        @pl.when(s < NCHUNK)
        def _():
            x_start(s + AHEAD)
            arrival = pltpu.make_async_remote_copy(
                src_ref=second.at[s], dst_ref=first.at[s], send_sem=xs.at[s], recv_sem=xr.at[s],
                device_id=(along_x, col), device_id_type=MESH)
            arrival.wait_recv()
            first[s] = first[s] + own[s]
            y_copy(s).start()

        k1 = s - HOP

        @pl.when(jnp.logical_and(k1 >= 0, k1 < NCHUNK))
        def _():
            y_copy(k1).wait_recv()
            second[k1] = second[k1] + first[k1]

            @pl.when(above == 0)
            def _():
                pass_on(second.at[k1], k1)
                left[core, k1] = second[k1]

        k2 = s - HOP * (1 + far)

        @pl.when(jnp.logical_and(far > 0, jnp.logical_and(k2 >= 0, k2 < NCHUNK)))
        def _():
            z_copy(second.at[k2], k2, partner, us).wait_recv()
            pass_on(left.at[core, k2], k2)

        k3 = s - LAG

        @pl.when(jnp.logical_and(k3 >= 0, k3 < NCHUNK))
        def _():
            pltpu.make_async_remote_copy(
                src_ref=second.at[k3], dst_ref=left.at[1 - core, k3], send_sem=ps.at[k3],
                recv_sem=pr.at[k3], device_id=(row, partner), device_id_type=MESH).wait_recv()

        @pl.when(s < nstrip)
        def _():
            strip_copy(s).wait()

            @pl.when(s + 1 < nstrip)
            def _():
                strip_copy(s + 1).start()

            value = strip[s % 2].astype(jnp.float32)
            energy[0] = energy[0] + jnp.sum((value * value).reshape(2 * STRIP // 8, 8, width), axis=0)

        step = s - (LAG + GROUP - 1)

        @pl.when(step >= 0)
        def _():
            group = step // GROUP
            part = step % GROUP

            @pl.when(part == 0)
            def _():
                re = second[pl.ds(group * GROUP, GROUP), 0]
                im = second[pl.ds(group * GROUP, GROUP), 1]
                right[0, :, 0] = re
                right[0, :, 1] = -im
                right[1, :, 0] = im
                right[1, :, 1] = re

            depth = 2 * GROUP * CHUNK
            per_half = width // TILE

            @pl.loop(0, 2 * per_half // GROUP)
            def _(i):
                tile = part * (2 * per_half // GROUP) + i
                half = tile // per_half
                inner = pl.multiple_of((tile % per_half) * TILE, TILE)
                at = pl.multiple_of(tile * TILE, TILE)
                lhs = left[half, pl.ds(group * GROUP, GROUP), :, :, pl.ds(inner, TILE)]
                lhs = lhs.reshape(depth, TILE)
                for c in range(2):
                    rhs = right[c].reshape(depth, width)
                    got = lax.dot_general(
                        lhs, rhs, (((0,), (0,)), ((), ())), preferred_element_type=jnp.float32)

                    @pl.when(group == 0)
                    def _():
                        acc[c, pl.ds(at, TILE), :] = got

                    @pl.when(jnp.logical_and(group > 0, group < NGROUP - 1))
                    def _():
                        acc[c, pl.ds(at, TILE), :] = acc[c, pl.ds(at, TILE), :] + got

                    @pl.when(group == NGROUP - 1)
                    def _():
                        value = (acc[c, pl.ds(at, TILE), :] + got) * factor
                        acc[c, pl.ds(at, TILE), :] = value
                        energy[1] = energy[1] + jnp.sum(
                            (value * value).reshape(TILE // 8, 8, width), axis=0)

                @pl.when(group == NGROUP - 1)
                def _():
                    for c in range(2):
                        out_copy(c, at).start()

    sums = energy[:, :, :128]
    for j in range(1, width // 128):
        sums = sums + energy[:, :, j * 128:(j + 1) * 128]
    part_sums[0] = sums

    @pl.loop(0, NCHUNK)
    def _(k):
        pltpu.make_async_remote_copy(
            src_ref=own.at[k], dst_ref=first.at[k], send_sem=xs.at[k], recv_sem=xr.at[k],
            device_id=(along_x, col), device_id_type=MESH).wait_send()
        y_copy(k).wait_send()
        p_copy(second.at[k], k).wait_send()

        @pl.when(go_up)
        def _():
            z_copy(second.at[k], k, col + 2, us).wait_send()

        @pl.when(go_down)
        def _():
            z_copy(second.at[k], k, col - 2, ds).wait_send()

    row_copies = [
        pltpu.make_async_remote_copy(
            src_ref=part_sums.at[0], dst_ref=row_sums.at[j - 1], send_sem=rs.at[j - 1],
            recv_sem=rr.at[j - 1], device_id=((row + j) % 4, col), device_id_type=MESH)
        for j in range(1, 4)
    ]
    for copy in row_copies:
        copy.start()
    for j in range(3):
        row_copies[j].wait_recv()
        sums = sums + row_sums[j]
    part_sums[1] = sums
    col_copies = [
        pltpu.make_async_remote_copy(
            src_ref=part_sums.at[1], dst_ref=col_sums.at[j - 1], send_sem=cs.at[j - 1],
            recv_sem=cr.at[j - 1], device_id=(row, (col + j) % 8), device_id_type=MESH)
        for j in range(1, 8)
    ]
    pltpu.make_async_copy(acc, mult, out_sem.at[0]).wait()
    for copy in col_copies:
        copy.start()
    for j in range(7):
        col_copies[j].wait_recv()
        sums = sums + col_sums[j]
    data = jnp.full((8, 128), jnp.sum(sums[0]), jnp.float32)
    predicted = jnp.full((8, 128), jnp.sum(sums[1]), jnp.float32)
    gain[...] = jnp.sqrt((data / count + 1e-05) / (predicted / count + 1e-05))
    for copy in row_copies + col_copies:
        copy.wait_send()


def local_fast(wavefield, panel_order, filter_taps):
    shot_block = wavefield.shape[2]
    recv_block = wavefield.shape[3]
    field = wavefield[:, 0]
    me = lax.axis_index("row")
    parts = []
    for t in range(STEPS):
        start = panel_order[t] * PANEL
        piece = lax.dynamic_slice_in_dim(field, start % shot_block, PANEL, 1)
        piece = jnp.where(me == start // shot_block, piece, jnp.zeros_like(piece))
        piece = piece.reshape(2, PANEL // CHUNK, CHUNK, recv_block)
        parts.append(jnp.swapaxes(piece, 0, 1))
    block = (NCHUNK, 2, CHUNK, recv_block)
    dma = pltpu.SemaphoreType.DMA
    def run(n, *args):
      return pl.pallas_call(
        functools.partial(predict_kernel, n),
        out_shape=(
            jax.ShapeDtypeStruct((2, shot_block, recv_block), jnp.float32),
            jax.ShapeDtypeStruct((8, 128), jnp.float32),
        ),
        in_specs=[pl.BlockSpec(memory_space=pl.ANY)] * 4,
        out_specs=(pl.BlockSpec(memory_space=pl.ANY), pl.BlockSpec(memory_space=pltpu.VMEM)),
        scratch_shapes=[
            pltpu.VMEM(block, jnp.bfloat16),
            pltpu.VMEM(block, jnp.bfloat16),
            pltpu.VMEM(block, jnp.bfloat16),
            pltpu.VMEM((2,) + block, jnp.bfloat16),
            pltpu.VMEM((2, shot_block, recv_block), jnp.float32),
            pltpu.VMEM((2, GROUP, 2, CHUNK, recv_block), jnp.bfloat16),
            pltpu.VMEM((2, 8, recv_block), jnp.float32),
            pltpu.VMEM((2, 2, STRIP, recv_block), jnp.bfloat16),
            pltpu.VMEM((2, 2, 8, 128), jnp.float32),
            pltpu.VMEM((3, 2, 8, 128), jnp.float32),
            pltpu.VMEM((7, 2, 8, 128), jnp.float32),
        ] + [dma((NCHUNK,))] * 9 + [
            dma((STEPS,)), dma((1,)), dma((2,)), dma((3,)), dma((3,)), dma((7,)), dma((7,))],
        compiler_params=pltpu.CompilerParams(
            collective_id=n, has_side_effects=True, vmem_limit_bytes=60 << 20),
        name="predict%d" % n,
    )(*args)
    owners = jnp.sort(panel_order[:STEPS] // 4)
    code = owners[0] * 16 + owners[1] * 4 + owners[2]
    branch = jnp.zeros((), jnp.int32)
    n = 0
    for i in range(4):
        for j in range(i, 4):
            for k in range(j, 4):
                branch = jnp.where(code == i * 16 + j * 4 + k, n, branch)
                n += 1
    mult, gain = lax.switch(branch, [functools.partial(run, m) for m in range(n)], *parts, field)
    scale = gain[0, 0]
    spec_re, spec_im = frequency_spectrum(filter_taps, 1)
    same = jnp.stack([spec_re, spec_re])
    cross = jnp.stack([-spec_im, spec_im])
    moved = scale * (same * mult + cross * mult[::-1])
    return (field.astype(jnp.float32) - moved).astype(jnp.bfloat16)[:, None]


def solution(mesh):
    in_specs = (P(None, None, "row", "col"), P(), P(None, "col"))
    out_specs = P(None, None, "row", "col")
    fast = mesh.shape["row"] == 4 and mesh.shape["col"] == 8
    body = local_fast if fast else local
    return jax.shard_map(body, mesh=mesh, in_specs=in_specs, out_specs=out_specs, check_vma=False)
```

```python
import math

import jax
import jax.numpy as jnp
from jax import lax
from jax.experimental import pallas as pl
from jax.experimental.pallas import tpu as pltpu
from jax.sharding import PartitionSpec as P

SIDE = 8192
PANEL = 512
STEPS = 3
TAPS = 11
FIRST_FREQUENCY = 8
NT = 1024
MESH = pl.DeviceIdType.MESH

CHUNK = 32
NCHUNK = STEPS * PANEL // CHUNK
GROUP = 256 // CHUNK
TILE = 512
LAST = GROUP
PACE = GROUP * TILE // 2048
HOP = 2
LAG = 7 * HOP
AHEAD = 2
STRIP = 64 // CHUNK
FINAL = 16
OUT = 256 // CHUNK
INNER = 6
INNER_AT = 3
OUTER = 24
OUTER_AT = (8, 20)
RELAYS = NCHUNK // INNER
LAST_PLANE = 3


def spread(block, axis, holder):
    block = jnp.where(lax.axis_index(axis) == holder, block, jnp.zeros_like(block))
    return lax.psum(block, axis)


def frequency_spectrum(filter_taps, freq_count):
    lags = jnp.arange(TAPS, dtype=jnp.float32)
    omega = 2.0 * math.pi * (FIRST_FREQUENCY + jnp.arange(freq_count, dtype=jnp.float32)) / NT
    phase = omega[:, None] * lags[None, :]
    real_part = jnp.dot(jnp.cos(phase), filter_taps, precision=lax.Precision.HIGHEST)
    imag_part = -jnp.dot(jnp.sin(phase), filter_taps, precision=lax.Precision.HIGHEST)
    return (real_part, imag_part)


def local(wavefield, panel_order, filter_taps):
    freq_count = wavefield.shape[1]
    shot_block = wavefield.shape[2]
    recv_block = wavefield.shape[3]
    own_row_index = lax.axis_index("row")
    factor = 1.0 / math.sqrt(STEPS * PANEL)
    count = 2.0 * SIDE * SIDE
    local_data = jnp.sum(jnp.square(wavefield.astype(jnp.float32)), axis=(0, 2, 3))
    energy_data = lax.psum(local_data, ("row", "col"))
    totals = jnp.zeros((freq_count, shot_block, 2 * recv_block), jnp.float32)
    for panel_advance in range(STEPS):
        first_point = panel_order[panel_advance] * PANEL
        row_width = min(PANEL, shot_block)
        owner_turn = 0
        start = first_point + owner_turn * row_width
        piece = lax.dynamic_slice_in_dim(wavefield, start % shot_block, row_width, 2)
        row_pieces = spread(piece, "row", start // shot_block)
        col_pieces = []
        mirror_width = min(shot_block, recv_block)
        for owner_turn in range(max(1, shot_block // recv_block)):
            start = own_row_index * shot_block + owner_turn * mirror_width
            piece = row_pieces
            col_pieces.append(spread(piece, "col", start // recv_block))
        upper = jnp.swapaxes(jnp.concatenate(col_pieces, axis=3), 2, 3)
        left_factor = jnp.concatenate([upper[0], upper[1]], axis=2)
        right_factor = jnp.concatenate(
            [
                jnp.concatenate([row_pieces[0], row_pieces[1]], axis=2),
                jnp.concatenate([-row_pieces[1], row_pieces[0]], axis=2),
            ],
            axis=1,
        )
        totals = totals + jnp.einsum(
            "yga,yah->ygh", left_factor, right_factor, preferred_element_type=jnp.float32
        )
    mult_re = totals[:, :, :recv_block] * factor
    mult_im = totals[:, :, recv_block:] * factor
    local_mult = jnp.sum(mult_re * mult_re, axis=(1, 2)) + jnp.sum(mult_im * mult_im, axis=(1, 2))
    energy_mult = lax.psum(local_mult, ("row", "col"))
    gain = jnp.sqrt((energy_data / count + 1e-05) / (energy_mult / count + 1e-05))[:, None, None]
    spec_re, spectrum_imaginary = frequency_spectrum(filter_taps, freq_count)
    a_re = spec_re[:, None, :]
    a_im = spectrum_imaginary[:, None, :]
    sub_re = gain * (a_re * mult_re - a_im * mult_im)
    subtracted_imaginary = gain * (a_re * mult_im + a_im * mult_re)
    result = jnp.stack(
        [
            wavefield[0].astype(jnp.float32) - sub_re,
            wavefield[1].astype(jnp.float32) - subtracted_imaginary,
        ]
    )
    return result.astype(jnp.bfloat16)


def predict_kernel(field, order, taps, result,
                   plane, own, right, in1, in2, left, acc, rhs, relay, energy, spec,
                   part_sums, row_sums, col_sums,
                   xs, xr, ys, yr, gs, gr, us, ds, zr, ps, pr, hs, hr, ns,
                   load_sem, out_sem, rs, rr, cs, cr):
    per_panel = PANEL // CHUNK
    count = 2.0 * SIDE * SIDE
    factor = 1.0 / math.sqrt(STEPS * PANEL)
    row = lax.axis_index("row")
    col = lax.axis_index("col")
    z = col // 2
    core = col % 2
    along_x = row + 1 - 2 * (row % 2)
    along_y = (row + 2) % 4
    partner = col + 1 - 2 * core
    blocks = plane.shape[1]
    shots = blocks * CHUNK
    width = plane.shape[3]
    per_block = shots // PANEL
    above = z - row
    far = jnp.abs(above)

    quarter = blocks // 4
    loads = [
        pltpu.make_async_copy(field.at[:, pl.ds(j * quarter, quarter)],
                              plane.at[:, pl.ds(j * quarter, quarter)], load_sem.at[j])
        for j in range(4)
    ]
    for load in loads:
        load.start()
    energy[...] = jnp.zeros_like(energy)

    @pl.loop(0, blocks)
    def _(i):
        here = pl.ds(pl.multiple_of(i * CHUNK, CHUNK), CHUNK)
        for c in range(2):
            acc[c, here, :] = jnp.zeros((CHUNK, width), jnp.float32)

    barrier = pltpu.get_barrier_semaphore()
    for j in range(1, 4):
        pl.semaphore_signal(barrier, inc=1, device_id=((row + j) % 4, col), device_id_type=MESH)
    for j in range(1, 8):
        pl.semaphore_signal(barrier, inc=1, device_id=(row, (col + j) % 8), device_id_type=MESH)
    re = jnp.zeros((1, width), jnp.float32)
    im = jnp.zeros((1, width), jnp.float32)
    for l in range(TAPS):
        phase = 2.0 * math.pi * FIRST_FREQUENCY / NT * l
        tap = taps[pl.ds(l, 1), :]
        re = re + math.cos(phase) * tap
        im = im - math.sin(phase) * tap
    spec[pl.ds(0, 1), :] = re
    spec[pl.ds(1, 1), :] = im
    pl.semaphore_wait(barrier, 10)

    def first_axis(k):
        return along_x + (k % 2) * (along_y - along_x)

    def second_axis(k):
        return along_y + (k % 2) * (along_x - along_y)

    def kept(k):
        return row % 2 + (k % 2) * (row // 2 - row % 2)

    def remote(src, dst, send, recv, to):
        return pltpu.make_async_remote_copy(
            src_ref=src, dst_ref=dst, send_sem=send, recv_sem=recv, device_id=to,
            device_id_type=MESH)

    def prepare(k):
        panel = order[k // per_panel]
        block = lax.rem(panel, per_block) * per_panel + k % per_panel
        mine = jnp.where(lax.div(panel, per_block) == row, 1.0, 0.0)
        for c in range(2):
            own[k, c] = (plane[c, block].astype(jnp.float32) * mine).astype(jnp.bfloat16)

    def give(k):
        return remote(own.at[k, 1 - kept(k)], in1.at[k], xs.at[0], xr.at[k], (first_axis(k), col))

    def swap(k):
        return remote(own.at[k, kept(k)], in2.at[k], ys.at[0], yr.at[k], (second_axis(k), col))

    def share(k, half):
        return remote(right.at[k, half], right.at[k, half], gs.at[0], gr.at[k],
                      (first_axis(k), col))

    def z_copy(src, k, to, sem):
        return remote(src, left.at[core, k], sem.at[0], zr.at[k], (row, to))

    def p_copy(src, k, half):
        return remote(src, left.at[half, k], ps.at[0], pr.at[k], (row, partner))

    def inner(k):
        return k % INNER == INNER_AT

    def outer(k, which):
        return k % OUTER == OUTER_AT[which]

    ways = []
    for way in range(2):
        at = row if way == 0 else LAST_PLANE - row
        level = z if way == 0 else LAST_PLANE - z
        to = col + 2 if way == 0 else col - 2
        ways.append((at, level, to, us if way == 0 else ds))

    def detoured(at, k):
        edge = jnp.logical_and(at == 0, jnp.logical_or(outer(k, 0), outer(k, 1)))
        return jnp.logical_or(edge, jnp.logical_and(jnp.logical_or(at == 1, at == 2), inner(k)))

    def sends(way, k):
        at, level, _, _ = ways[way]
        return jnp.logical_and(jnp.logical_and(level >= at, level < LAST_PLANE),
                               jnp.logical_not(detoured(at, k)))

    def pass_on(src, k):
        for way in range(2):
            @pl.when(sends(way, k))
            def _():
                z_copy(src, k, ways[way][2], ways[way][3]).start()

    carried = []
    for way in range(2):
        for carrier, source, to in ((1, 0, along_x), (2, 0, along_y), (3, 1, along_y), (3, 2, along_x)):
            slot = source - 1 if carrier == 3 else way
            carried.append((way, carrier, source, to, slot))

    def taken(entry, k):
        carrier = entry[1]
        return inner(k) if carrier == 3 else outer(k, carrier - 1)

    def place(entry, k):
        return k // INNER if entry[1] == 3 else k // OUTER

    def hop(entry, src, k):
        way, _, _, _, slot = entry
        n = place(entry, k)
        return remote(src, relay.at[slot, n], hs.at[slot], hr.at[slot, n], (row, ways[way][2]))

    def deliver(entry, k):
        _, _, _, to, slot = entry
        n = place(entry, k)
        return remote(relay.at[slot, n], left.at[core, k], ns.at[slot], zr.at[k], (to, col))

    def carrying(entry, k):
        return jnp.logical_and(ways[entry[0]][0] == entry[1],
                               jnp.logical_and(jnp.logical_and(k >= 0, k < NCHUNK), taken(entry, k)))

    def build(at, size):
        re = right[pl.ds(at, size), 0]
        im = right[pl.ds(at, size), 1]
        rhs[0, pl.ds(0, size), 0] = re
        rhs[0, pl.ds(0, size), 1] = -im
        rhs[1, pl.ds(0, size), 0] = im
        rhs[1, pl.ds(0, size), 1] = re

    def product(at, size, tile, c):
        per_half = width // TILE
        depth = 2 * size * CHUNK
        inside = pl.multiple_of((tile % per_half) * TILE, TILE)
        lhs = left[tile // per_half, pl.ds(at, size), :, :, pl.ds(inside, TILE)]
        return lax.dot_general(
            lhs.reshape(depth, TILE), rhs[c, pl.ds(0, size)].reshape(depth, width),
            (((0,), (0,)), ((), ())), preferred_element_type=jnp.float32)

    for load in loads:
        load.wait()

    @pl.loop(0, AHEAD)
    def _(k):
        prepare(k)
        give(k).start()

    @pl.loop(0, NCHUNK + LAG)
    def _(s):
        @pl.when(s + AHEAD < NCHUNK)
        def _():
            prepare(s + AHEAD)
            give(s + AHEAD).start()

        @pl.when(s < NCHUNK)
        def _():
            give(s).wait_recv()
            own[s, kept(s)] = own[s, kept(s)] + in1[s]
            swap(s).start()

        k1 = s - HOP

        @pl.when(jnp.logical_and(k1 >= 0, k1 < NCHUNK))
        def _():
            swap(k1).wait_recv()
            right[k1, kept(k1)] = own[k1, kept(k1)] + in2[k1]
            share(k1, kept(k1)).start()

        k2 = s - 2 * HOP

        @pl.when(jnp.logical_and(k2 >= 0, k2 < NCHUNK))
        def _():
            share(k2, 1 - kept(k2)).wait_recv()

            @pl.when(above == 0)
            def _():
                pass_on(right.at[k2], k2)
                p_copy(right.at[k2], k2, core).start()
                left[core, k2] = right[k2]

        for entry in carried:
            @pl.when(jnp.logical_and(carrying(entry, k2), ways[entry[0]][1] == entry[2]))
            def _():
                hop(entry, right.at[k2], k2).start()

        k3 = s - HOP * (2 + far)
        toward = jnp.where(above > 0, row, LAST_PLANE - row)

        @pl.when(jnp.logical_and(jnp.logical_and(far > 0, jnp.logical_not(detoured(toward, k3))),
                                 jnp.logical_and(k3 >= 0, k3 < NCHUNK)))
        def _():
            z_copy(right.at[k3], k3, partner, us).wait_recv()
            pass_on(left.at[core, k3], k3)
            p_copy(left.at[core, k3], k3, core).start()

        for entry in carried:
            way, _, source, _, slot = entry
            level = ways[way][1]
            k4 = s - HOP * (2 + level - source)

            @pl.when(jnp.logical_and(carrying(entry, k4), level > source))
            def _():
                hop(entry, right.at[k4], k4).wait_recv()
                deliver(entry, k4).start()

                @pl.when(level < LAST_PLANE)
                def _():
                    hop(entry, relay.at[slot, place(entry, k4)], k4).start()

        k5 = s - HOP * (3 + far)

        @pl.when(jnp.logical_and(jnp.logical_and(far > 0, detoured(toward, k5)),
                                 jnp.logical_and(k5 >= 0, k5 < NCHUNK)))
        def _():
            z_copy(right.at[k5], k5, partner, us).wait_recv()
            p_copy(left.at[core, k5], k5, core).start()

        k6 = s - LAG

        @pl.when(jnp.logical_and(k6 >= 0, k6 < NCHUNK))
        def _():
            p_copy(right.at[k6], k6, 1 - core).wait_recv()

        @pl.when(s < blocks // STRIP)
        def _():
            for c in range(2):
                value = plane[c, pl.ds(s * STRIP, STRIP)].astype(jnp.float32)
                energy[0] = energy[0] + jnp.sum(
                    (value * value).reshape(STRIP * CHUNK // 8, 8, width), axis=0)

        step = s - (LAG + GROUP - 1)

        @pl.when(jnp.logical_and(step >= 0, step < NCHUNK - LAST))
        def _():
            part = step % GROUP
            at_chunk = step - part

            @pl.when(part == 0)
            def _():
                build(at_chunk, GROUP)

            @pl.when(part % PACE == 0)
            def _():
                tile = part // PACE
                for c in range(2):
                    here = pl.ds(pl.multiple_of(tile * TILE, TILE), TILE)
                    acc[c, here, :] = acc[c, here, :] + product(at_chunk, GROUP, tile, c)

    build(NCHUNK - LAST, LAST)

    @pl.loop(0, shots // TILE)
    def _(tile):
        for c in range(2):
            here = pl.ds(pl.multiple_of(tile * TILE, TILE), TILE)
            value = (acc[c, here, :] + product(NCHUNK - LAST, LAST, tile, c)) * factor
            acc[c, here, :] = value
            energy[1] = energy[1] + jnp.sum((value * value).reshape(TILE // 8, 8, width), axis=0)

    sums = energy[:, :, :128]
    for j in range(1, width // 128):
        sums = sums + energy[:, :, j * 128:(j + 1) * 128]
    part_sums[0] = sums
    row_copies = [
        remote(part_sums.at[0], row_sums.at[j - 1], rs.at[j - 1], rr.at[j - 1], ((row + j) % 4, col))
        for j in range(1, 4)
    ]
    for copy in row_copies:
        copy.start()

    for sem in (xs, ys, gs):
        remote(in1, in2, sem.at[0], xr.at[0], (along_x, col)).wait_send()
    remote(left.at[core], left.at[core], ps.at[0], pr.at[0], (row, partner)).wait_send()
    for way in range(2):
        at, level, _, sem = ways[way]
        for first, last, detours in ((0, 1, 2 * NCHUNK // OUTER), (1, LAST_PLANE, RELAYS)):
            part = left.at[core, pl.ds(0, NCHUNK - detours)]

            @pl.when(jnp.logical_and(jnp.logical_and(at >= first, at < last),
                                     jnp.logical_and(level >= at, level < LAST_PLANE)))
            def _():
                remote(part, part, sem.at[0], zr.at[0], (row, partner)).wait_send()
    for entry in carried:
        level = ways[entry[0]][1]
        part = relay.at[entry[4], pl.ds(0, RELAYS if entry[1] == 3 else NCHUNK // OUTER)]

        @pl.when(jnp.logical_and(ways[entry[0]][0] == entry[1], level > entry[2]))
        def _():
            remote(part, part, ns.at[entry[4]], zr.at[0], (row, partner)).wait_send()

        @pl.when(jnp.logical_and(ways[entry[0]][0] == entry[1],
                                 jnp.logical_and(level >= entry[2], level < LAST_PLANE)))
        def _():
            remote(part, part, hs.at[entry[4]], zr.at[0], (row, partner)).wait_send()

    for j in range(3):
        row_copies[j].wait_recv()
        sums = sums + row_sums[j]
    part_sums[1] = sums
    col_copies = [
        remote(part_sums.at[1], col_sums.at[j - 1], cs.at[j - 1], cr.at[j - 1], (row, (col + j) % 8))
        for j in range(1, 8)
    ]
    for copy in col_copies:
        copy.start()
    for j in range(7):
        col_copies[j].wait_recv()
        sums = sums + col_sums[j]
    data = jnp.full((1, width), jnp.sum(sums[0]), jnp.float32)
    predicted = jnp.full((1, width), jnp.sum(sums[1]), jnp.float32)
    gain = jnp.sqrt((data / count + 1e-05) / (predicted / count + 1e-05))
    re = gain * spec[pl.ds(0, 1), :]
    im = gain * spec[pl.ds(1, 1), :]

    def out_copy(i):
        part = pl.ds(i * OUT, OUT)
        return pltpu.make_async_copy(plane.at[:, part], result.at[:, part], out_sem.at[i])

    @pl.loop(0, blocks // OUT)
    def _(i):
        @pl.loop(i * OUT, (i + 1) * OUT)
        def _(j):
            for half in range(CHUNK // FINAL):
                rows = slice(half * FINAL, (half + 1) * FINAL)
                here = pl.ds(pl.multiple_of(j * CHUNK + half * FINAL, FINAL), FINAL)
                mult_re = acc[0, here, :]
                mult_im = acc[1, here, :]
                plane[0, j, rows] = (plane[0, j, rows].astype(jnp.float32)
                                     - (re * mult_re - im * mult_im)).astype(jnp.bfloat16)
                plane[1, j, rows] = (plane[1, j, rows].astype(jnp.float32)
                                     - (re * mult_im + im * mult_re)).astype(jnp.bfloat16)

        out_copy(i).start()

    for copy in row_copies + col_copies:
        copy.wait_send()

    @pl.loop(0, blocks // OUT)
    def _(i):
        out_copy(i).wait()


def local_fast(wavefield, panel_order, filter_taps):
    shot_block = wavefield.shape[2]
    recv_block = wavefield.shape[3]
    block = (NCHUNK, 2, CHUNK, recv_block)
    whole = (2, shot_block // CHUNK, CHUNK, recv_block)
    dma = pltpu.SemaphoreType.DMA
    vmem = pltpu.VMEM
    result = pl.pallas_call(
        predict_kernel,
        out_shape=jax.ShapeDtypeStruct(whole, jnp.bfloat16),
        in_specs=[
            pl.BlockSpec(memory_space=pl.ANY),
            pl.BlockSpec(memory_space=pltpu.SMEM),
            pl.BlockSpec(memory_space=pltpu.VMEM),
        ],
        out_specs=pl.BlockSpec(memory_space=pl.ANY),
        scratch_shapes=[
            vmem(whole, jnp.bfloat16),
            vmem(block, jnp.bfloat16),
            vmem(block, jnp.bfloat16),
            vmem((NCHUNK, CHUNK, recv_block), jnp.bfloat16),
            vmem((NCHUNK, CHUNK, recv_block), jnp.bfloat16),
            vmem((2,) + block, jnp.bfloat16),
            vmem((2, shot_block, recv_block), jnp.float32),
            vmem((2, GROUP, 2, CHUNK, recv_block), jnp.bfloat16),
            vmem((2, RELAYS, 2, CHUNK, recv_block), jnp.bfloat16),
            vmem((2, 8, recv_block), jnp.float32),
            vmem((8, recv_block), jnp.float32),
            vmem((2, 2, 8, 128), jnp.float32),
            vmem((3, 2, 8, 128), jnp.float32),
            vmem((7, 2, 8, 128), jnp.float32),
        ] + [dma((1,)), dma((NCHUNK,))] * 3 + [dma((1,)), dma((1,)), dma((NCHUNK,))] + [
            dma((1,)), dma((NCHUNK,)), dma((2,)), dma((2, RELAYS)), dma((2,)),
            dma((4,)), dma((shot_block // CHUNK // OUT,)), dma((3,)), dma((3,)), dma((7,)), dma((7,))],
        compiler_params=pltpu.CompilerParams(
            collective_id=0, has_side_effects=True, vmem_limit_bytes=62 << 20),
        name="predict",
    )(wavefield.reshape(whole), panel_order, filter_taps)
    return result.reshape(wavefield.shape)


def solution(mesh):
    in_specs = (P(None, None, "row", "col"), P(), P(None, "col"))
    out_specs = P(None, None, "row", "col")
    fast = mesh.shape["row"] == 4 and mesh.shape["col"] == 8
    body = local_fast if fast else local
    return jax.shard_map(body, mesh=mesh, in_specs=in_specs, out_specs=out_specs, check_vma=False)
```

```python
import math

import jax
import jax.numpy as jnp
from jax import lax
from jax.experimental import pallas as pl
from jax.experimental.pallas import tpu as pltpu
from jax.sharding import PartitionSpec as P

SIDE = 8192
PANEL = 512
STEPS = 3
TAPS = 11
FIRST_FREQUENCY = 8
NT = 1024
MESH = pl.DeviceIdType.MESH

CHUNK = 32
NCHUNK = STEPS * PANEL // CHUNK
GROUP = 128 // CHUNK
TILE = 512
LAST = GROUP
PACE = GROUP * TILE // 2048
HOP = 2
LAG = 7 * HOP
AHEAD = 2
STRIP = 64 // CHUNK
FINAL = 16
INNER = 6
INNER_AT = 3
OUTER = 24
OUTER_AT = (8, 20)
RELAYS = NCHUNK // INNER
LAST_PLANE = 3


def spread(block, axis, holder):
    block = jnp.where(lax.axis_index(axis) == holder, block, jnp.zeros_like(block))
    return lax.psum(block, axis)


def frequency_spectrum(filter_taps, freq_count):
    lags = jnp.arange(TAPS, dtype=jnp.float32)
    omega = 2.0 * math.pi * (FIRST_FREQUENCY + jnp.arange(freq_count, dtype=jnp.float32)) / NT
    phase = omega[:, None] * lags[None, :]
    real_part = jnp.dot(jnp.cos(phase), filter_taps, precision=lax.Precision.HIGHEST)
    imag_part = -jnp.dot(jnp.sin(phase), filter_taps, precision=lax.Precision.HIGHEST)
    return (real_part, imag_part)


def local(wavefield, panel_order, filter_taps):
    freq_count = wavefield.shape[1]
    shot_block = wavefield.shape[2]
    recv_block = wavefield.shape[3]
    own_row_index = lax.axis_index("row")
    factor = 1.0 / math.sqrt(STEPS * PANEL)
    count = 2.0 * SIDE * SIDE
    local_data = jnp.sum(jnp.square(wavefield.astype(jnp.float32)), axis=(0, 2, 3))
    energy_data = lax.psum(local_data, ("row", "col"))
    totals = jnp.zeros((freq_count, shot_block, 2 * recv_block), jnp.float32)
    for panel_advance in range(STEPS):
        first_point = panel_order[panel_advance] * PANEL
        row_width = min(PANEL, shot_block)
        owner_turn = 0
        start = first_point + owner_turn * row_width
        piece = lax.dynamic_slice_in_dim(wavefield, start % shot_block, row_width, 2)
        row_pieces = spread(piece, "row", start // shot_block)
        col_pieces = []
        mirror_width = min(shot_block, recv_block)
        for owner_turn in range(max(1, shot_block // recv_block)):
            start = own_row_index * shot_block + owner_turn * mirror_width
            piece = row_pieces
            col_pieces.append(spread(piece, "col", start // recv_block))
        upper = jnp.swapaxes(jnp.concatenate(col_pieces, axis=3), 2, 3)
        left_factor = jnp.concatenate([upper[0], upper[1]], axis=2)
        right_factor = jnp.concatenate(
            [
                jnp.concatenate([row_pieces[0], row_pieces[1]], axis=2),
                jnp.concatenate([-row_pieces[1], row_pieces[0]], axis=2),
            ],
            axis=1,
        )
        totals = totals + jnp.einsum(
            "yga,yah->ygh", left_factor, right_factor, preferred_element_type=jnp.float32
        )
    mult_re = totals[:, :, :recv_block] * factor
    mult_im = totals[:, :, recv_block:] * factor
    local_mult = jnp.sum(mult_re * mult_re, axis=(1, 2)) + jnp.sum(mult_im * mult_im, axis=(1, 2))
    energy_mult = lax.psum(local_mult, ("row", "col"))
    gain = jnp.sqrt((energy_data / count + 1e-05) / (energy_mult / count + 1e-05))[:, None, None]
    spec_re, spectrum_imaginary = frequency_spectrum(filter_taps, freq_count)
    a_re = spec_re[:, None, :]
    a_im = spectrum_imaginary[:, None, :]
    sub_re = gain * (a_re * mult_re - a_im * mult_im)
    subtracted_imaginary = gain * (a_re * mult_im + a_im * mult_re)
    result = jnp.stack(
        [
            wavefield[0].astype(jnp.float32) - sub_re,
            wavefield[1].astype(jnp.float32) - subtracted_imaginary,
        ]
    )
    return result.astype(jnp.bfloat16)


def predict_kernel(field, order, taps, plane,
                   own, right, in1, in2, left, acc, rhs, relay, energy, spec,
                   part_sums, row_sums, col_sums,
                   xs, xr, ys, yr, gs, gr, us, ds, zr, ps, pr, hs, hr, ns,
                   load_sem, rs, rr, cs, cr):
    per_panel = PANEL // CHUNK
    count = 2.0 * SIDE * SIDE
    factor = 1.0 / math.sqrt(STEPS * PANEL)
    row = lax.axis_index("row")
    col = lax.axis_index("col")
    z = col // 2
    core = col % 2
    along_x = row + 1 - 2 * (row % 2)
    along_y = (row + 2) % 4
    partner = col + 1 - 2 * core
    blocks = plane.shape[1]
    shots = blocks * CHUNK
    width = plane.shape[3]
    per_block = shots // PANEL
    above = z - row
    far = jnp.abs(above)

    quarter = blocks // 4
    loads = [
        pltpu.make_async_copy(field.at[:, pl.ds(j * quarter, quarter)],
                              plane.at[:, pl.ds(j * quarter, quarter)], load_sem.at[j])
        for j in range(4)
    ]
    for load in loads:
        load.start()
    energy[...] = jnp.zeros_like(energy)

    @pl.loop(0, blocks)
    def _(i):
        here = pl.ds(pl.multiple_of(i * CHUNK, CHUNK), CHUNK)
        for c in range(2):
            acc[c, here, :] = jnp.zeros((CHUNK, width), jnp.float32)

    barrier = pltpu.get_barrier_semaphore()
    for j in range(1, 4):
        pl.semaphore_signal(barrier, inc=1, device_id=((row + j) % 4, col), device_id_type=MESH)
    for j in range(1, 8):
        pl.semaphore_signal(barrier, inc=1, device_id=(row, (col + j) % 8), device_id_type=MESH)
    re = jnp.zeros((1, width), jnp.float32)
    im = jnp.zeros((1, width), jnp.float32)
    for l in range(TAPS):
        phase = 2.0 * math.pi * FIRST_FREQUENCY / NT * l
        tap = taps[pl.ds(l, 1), :]
        re = re + math.cos(phase) * tap
        im = im - math.sin(phase) * tap
    spec[pl.ds(0, 1), :] = re
    spec[pl.ds(1, 1), :] = im
    pl.semaphore_wait(barrier, 10)

    def first_axis(k):
        return along_x + (k % 2) * (along_y - along_x)

    def second_axis(k):
        return along_y + (k % 2) * (along_x - along_y)

    def kept(k):
        return row % 2 + (k % 2) * (row // 2 - row % 2)

    def remote(src, dst, send, recv, to):
        return pltpu.make_async_remote_copy(
            src_ref=src, dst_ref=dst, send_sem=send, recv_sem=recv, device_id=to,
            device_id_type=MESH)

    def prepare(k):
        panel = order[k // per_panel]
        block = lax.rem(panel, per_block) * per_panel + k % per_panel
        mine = jnp.where(lax.div(panel, per_block) == row, 1.0, 0.0)
        for c in range(2):
            own[k, c] = (plane[c, block].astype(jnp.float32) * mine).astype(jnp.bfloat16)

    def give(k):
        return remote(own.at[k, 1 - kept(k)], in1.at[k], xs.at[0], xr.at[k], (first_axis(k), col))

    def swap(k):
        return remote(own.at[k, kept(k)], in2.at[k], ys.at[0], yr.at[k], (second_axis(k), col))

    def share(k, half):
        return remote(right.at[k, half], right.at[k, half], gs.at[0], gr.at[k],
                      (first_axis(k), col))

    def z_copy(src, k, to, sem):
        return remote(src, left.at[core, k], sem.at[0], zr.at[k], (row, to))

    def p_copy(src, k, half):
        return remote(src, left.at[half, k], ps.at[0], pr.at[k], (row, partner))

    def inner(k):
        return k % INNER == INNER_AT

    def outer(k, which):
        return k % OUTER == OUTER_AT[which]

    ways = []
    for way in range(2):
        at = row if way == 0 else LAST_PLANE - row
        level = z if way == 0 else LAST_PLANE - z
        to = col + 2 if way == 0 else col - 2
        ways.append((at, level, to, us if way == 0 else ds))

    def detoured(at, k):
        edge = jnp.logical_and(at == 0, jnp.logical_or(outer(k, 0), outer(k, 1)))
        return jnp.logical_or(edge, jnp.logical_and(jnp.logical_or(at == 1, at == 2), inner(k)))

    def sends(way, k):
        at, level, _, _ = ways[way]
        return jnp.logical_and(jnp.logical_and(level >= at, level < LAST_PLANE),
                               jnp.logical_not(detoured(at, k)))

    def pass_on(src, k):
        for way in range(2):
            @pl.when(sends(way, k))
            def _():
                z_copy(src, k, ways[way][2], ways[way][3]).start()

    carried = []
    for way in range(2):
        for carrier, source, to in ((1, 0, along_x), (2, 0, along_y), (3, 1, along_y), (3, 2, along_x)):
            slot = source - 1 if carrier == 3 else way
            carried.append((way, carrier, source, to, slot))

    def taken(entry, k):
        carrier = entry[1]
        return inner(k) if carrier == 3 else outer(k, carrier - 1)

    def place(entry, k):
        return k // INNER if entry[1] == 3 else k // OUTER

    def hop(entry, src, k):
        way, _, _, _, slot = entry
        n = place(entry, k)
        return remote(src, relay.at[slot, n], hs.at[slot], hr.at[slot, n], (row, ways[way][2]))

    def deliver(entry, k):
        _, _, _, to, slot = entry
        n = place(entry, k)
        return remote(relay.at[slot, n], left.at[core, k], ns.at[slot], zr.at[k], (to, col))

    def carrying(entry, k):
        return jnp.logical_and(ways[entry[0]][0] == entry[1],
                               jnp.logical_and(jnp.logical_and(k >= 0, k < NCHUNK), taken(entry, k)))

    def build(at, size):
        re = right[pl.ds(at, size), 0]
        im = right[pl.ds(at, size), 1]
        rhs[0, pl.ds(0, size), 0] = re
        rhs[0, pl.ds(0, size), 1] = -im
        rhs[1, pl.ds(0, size), 0] = im
        rhs[1, pl.ds(0, size), 1] = re

    def product(at, size, tile, c):
        per_half = width // TILE
        depth = 2 * size * CHUNK
        inside = pl.multiple_of((tile % per_half) * TILE, TILE)
        lhs = left[tile // per_half, pl.ds(at, size), :, :, pl.ds(inside, TILE)]
        return lax.dot_general(
            lhs.reshape(depth, TILE), rhs[c, pl.ds(0, size)].reshape(depth, width),
            (((0,), (0,)), ((), ())), preferred_element_type=jnp.float32)

    for load in loads:
        load.wait()

    @pl.loop(0, AHEAD)
    def _(k):
        prepare(k)
        give(k).start()

    @pl.loop(0, NCHUNK + LAG)
    def _(s):
        @pl.when(s + AHEAD < NCHUNK)
        def _():
            prepare(s + AHEAD)
            give(s + AHEAD).start()

        @pl.when(s < NCHUNK)
        def _():
            give(s).wait_recv()
            own[s, kept(s)] = own[s, kept(s)] + in1[s]
            swap(s).start()

        k1 = s - HOP

        @pl.when(jnp.logical_and(k1 >= 0, k1 < NCHUNK))
        def _():
            swap(k1).wait_recv()
            right[k1, kept(k1)] = own[k1, kept(k1)] + in2[k1]
            share(k1, kept(k1)).start()

        k2 = s - 2 * HOP

        @pl.when(jnp.logical_and(k2 >= 0, k2 < NCHUNK))
        def _():
            share(k2, 1 - kept(k2)).wait_recv()

            @pl.when(above == 0)
            def _():
                pass_on(right.at[k2], k2)
                p_copy(right.at[k2], k2, core).start()
                left[core, k2] = right[k2]

        for entry in carried:
            @pl.when(jnp.logical_and(carrying(entry, k2), ways[entry[0]][1] == entry[2]))
            def _():
                hop(entry, right.at[k2], k2).start()

        k3 = s - HOP * (2 + far)
        toward = jnp.where(above > 0, row, LAST_PLANE - row)

        @pl.when(jnp.logical_and(jnp.logical_and(far > 0, jnp.logical_not(detoured(toward, k3))),
                                 jnp.logical_and(k3 >= 0, k3 < NCHUNK)))
        def _():
            z_copy(right.at[k3], k3, partner, us).wait_recv()
            pass_on(left.at[core, k3], k3)
            p_copy(left.at[core, k3], k3, core).start()

        for entry in carried:
            way, _, source, _, slot = entry
            level = ways[way][1]
            k4 = s - HOP * (2 + level - source)

            @pl.when(jnp.logical_and(carrying(entry, k4), level > source))
            def _():
                hop(entry, right.at[k4], k4).wait_recv()
                deliver(entry, k4).start()

                @pl.when(level < LAST_PLANE)
                def _():
                    hop(entry, relay.at[slot, place(entry, k4)], k4).start()

        k5 = s - HOP * (3 + far)

        @pl.when(jnp.logical_and(jnp.logical_and(far > 0, detoured(toward, k5)),
                                 jnp.logical_and(k5 >= 0, k5 < NCHUNK)))
        def _():
            z_copy(right.at[k5], k5, partner, us).wait_recv()
            p_copy(left.at[core, k5], k5, core).start()

        k6 = s - LAG

        @pl.when(jnp.logical_and(k6 >= 0, k6 < NCHUNK))
        def _():
            p_copy(right.at[k6], k6, 1 - core).wait_recv()

        @pl.when(s < blocks // STRIP)
        def _():
            for c in range(2):
                value = plane[c, pl.ds(s * STRIP, STRIP)].astype(jnp.float32)
                energy[0] = energy[0] + jnp.sum(
                    (value * value).reshape(STRIP * CHUNK // 8, 8, width), axis=0)

        step = s - (LAG + GROUP - 1)

        @pl.when(jnp.logical_and(step >= 0, step < NCHUNK - LAST))
        def _():
            part = step % GROUP
            at_chunk = step - part

            @pl.when(part == 0)
            def _():
                build(at_chunk, GROUP)

            @pl.when(part % PACE == 0)
            def _():
                tile = part // PACE
                for c in range(2):
                    here = pl.ds(pl.multiple_of(tile * TILE, TILE), TILE)
                    acc[c, here, :] = acc[c, here, :] + product(at_chunk, GROUP, tile, c)

    build(NCHUNK - LAST, LAST)

    @pl.loop(0, shots // TILE)
    def _(tile):
        for c in range(2):
            here = pl.ds(pl.multiple_of(tile * TILE, TILE), TILE)
            value = (acc[c, here, :] + product(NCHUNK - LAST, LAST, tile, c)) * factor
            acc[c, here, :] = value
            energy[1] = energy[1] + jnp.sum((value * value).reshape(TILE // 8, 8, width), axis=0)

    sums = energy[:, :, :128]
    for j in range(1, width // 128):
        sums = sums + energy[:, :, j * 128:(j + 1) * 128]
    part_sums[0] = sums
    row_copies = [
        remote(part_sums.at[0], row_sums.at[j - 1], rs.at[j - 1], rr.at[j - 1], ((row + j) % 4, col))
        for j in range(1, 4)
    ]
    for copy in row_copies:
        copy.start()

    for sem in (xs, ys, gs):
        remote(in1, in2, sem.at[0], xr.at[0], (along_x, col)).wait_send()
    remote(left.at[core], left.at[core], ps.at[0], pr.at[0], (row, partner)).wait_send()
    for way in range(2):
        at, level, _, sem = ways[way]
        for first, last, detours in ((0, 1, 2 * NCHUNK // OUTER), (1, LAST_PLANE, RELAYS)):
            part = left.at[core, pl.ds(0, NCHUNK - detours)]

            @pl.when(jnp.logical_and(jnp.logical_and(at >= first, at < last),
                                     jnp.logical_and(level >= at, level < LAST_PLANE)))
            def _():
                remote(part, part, sem.at[0], zr.at[0], (row, partner)).wait_send()
    for entry in carried:
        level = ways[entry[0]][1]
        part = relay.at[entry[4], pl.ds(0, RELAYS if entry[1] == 3 else NCHUNK // OUTER)]

        @pl.when(jnp.logical_and(ways[entry[0]][0] == entry[1], level > entry[2]))
        def _():
            remote(part, part, ns.at[entry[4]], zr.at[0], (row, partner)).wait_send()

        @pl.when(jnp.logical_and(ways[entry[0]][0] == entry[1],
                                 jnp.logical_and(level >= entry[2], level < LAST_PLANE)))
        def _():
            remote(part, part, hs.at[entry[4]], zr.at[0], (row, partner)).wait_send()

    for j in range(3):
        row_copies[j].wait_recv()
        sums = sums + row_sums[j]
    part_sums[1] = sums
    col_copies = [
        remote(part_sums.at[1], col_sums.at[j - 1], cs.at[j - 1], cr.at[j - 1], (row, (col + j) % 8))
        for j in range(1, 8)
    ]
    for copy in col_copies:
        copy.start()
    for j in range(7):
        col_copies[j].wait_recv()
        sums = sums + col_sums[j]
    data = jnp.full((1, width), jnp.sum(sums[0]), jnp.float32)
    predicted = jnp.full((1, width), jnp.sum(sums[1]), jnp.float32)
    gain = jnp.sqrt((data / count + 1e-05) / (predicted / count + 1e-05))
    re = gain * spec[pl.ds(0, 1), :]
    im = gain * spec[pl.ds(1, 1), :]

    @pl.loop(0, blocks)
    def _(j):
        for half in range(CHUNK // FINAL):
            rows = slice(half * FINAL, (half + 1) * FINAL)
            here = pl.ds(pl.multiple_of(j * CHUNK + half * FINAL, FINAL), FINAL)
            mult_re = acc[0, here, :]
            mult_im = acc[1, here, :]
            plane[0, j, rows] = (plane[0, j, rows].astype(jnp.float32)
                                  - (re * mult_re - im * mult_im)).astype(jnp.bfloat16)
            plane[1, j, rows] = (plane[1, j, rows].astype(jnp.float32)
                                  - (re * mult_im + im * mult_re)).astype(jnp.bfloat16)

    for copy in row_copies + col_copies:
        copy.wait_send()


def local_fast(wavefield, panel_order, filter_taps):
    shot_block = wavefield.shape[2]
    recv_block = wavefield.shape[3]
    block = (NCHUNK, 2, CHUNK, recv_block)
    whole = (2, shot_block // CHUNK, CHUNK, recv_block)
    dma = pltpu.SemaphoreType.DMA
    vmem = pltpu.VMEM
    result = pl.pallas_call(
        predict_kernel,
        out_shape=pltpu.VMEM(whole, jnp.bfloat16),
        in_specs=[
            pl.BlockSpec(memory_space=pl.ANY),
            pl.BlockSpec(memory_space=pltpu.SMEM),
            pl.BlockSpec(memory_space=pltpu.VMEM),
        ],
        out_specs=pl.BlockSpec(memory_space=pltpu.VMEM),
        scratch_shapes=[
            vmem(block, jnp.bfloat16),
            vmem(block, jnp.bfloat16),
            vmem((NCHUNK, CHUNK, recv_block), jnp.bfloat16),
            vmem((NCHUNK, CHUNK, recv_block), jnp.bfloat16),
            vmem((2,) + block, jnp.bfloat16),
            vmem((2, shot_block, recv_block), jnp.float32),
            vmem((2, GROUP, 2, CHUNK, recv_block), jnp.bfloat16),
            vmem((2, RELAYS, 2, CHUNK, recv_block), jnp.bfloat16),
            vmem((2, 8, recv_block), jnp.float32),
            vmem((8, recv_block), jnp.float32),
            vmem((2, 2, 8, 128), jnp.float32),
            vmem((3, 2, 8, 128), jnp.float32),
            vmem((7, 2, 8, 128), jnp.float32),
        ] + [dma((1,)), dma((NCHUNK,))] * 3 + [dma((1,)), dma((1,)), dma((NCHUNK,))] + [
            dma((1,)), dma((NCHUNK,)), dma((2,)), dma((2, RELAYS)), dma((2,)),
            dma((4,)), dma((3,)), dma((3,)), dma((7,)), dma((7,))],
        compiler_params=pltpu.CompilerParams(
            collective_id=0, has_side_effects=True, vmem_limit_bytes=52 << 20),
        name="predict",
    )(wavefield.reshape(whole), panel_order, filter_taps)
    return result.reshape(wavefield.shape)


def solution(mesh):
    in_specs = (P(None, None, "row", "col"), P(), P(None, "col"))
    out_specs = P(None, None, "row", "col")
    fast = mesh.shape["row"] == 4 and mesh.shape["col"] == 8
    body = local_fast if fast else local
    return jax.shard_map(body, mesh=mesh, in_specs=in_specs, out_specs=out_specs, check_vma=False)
```

```python
import math

import jax
import jax.numpy as jnp
from jax import lax
from jax.experimental import pallas as pl
from jax.experimental.pallas import tpu as pltpu
from jax.sharding import PartitionSpec as P

SIDE = 8192
PANEL = 512
STEPS = 3
TAPS = 11
FIRST_FREQUENCY = 8
NT = 1024
MESH = pl.DeviceIdType.MESH

CHUNK = 32
NCHUNK = STEPS * PANEL // CHUNK
GROUP = 128 // CHUNK
TILE = 512
LAST = GROUP
PACE = GROUP * TILE // 2048
HOP = 2
LAG = 6 * HOP + 1
AHEAD = 2
STRIP = 64 // CHUNK
FINAL = 16
INNER = 6
INNER_AT = 3
OUTER = 24
OUTER_AT = (8, 20)
RELAYS = NCHUNK // INNER
LAST_PLANE = 3


def spread(block, axis, holder):
    block = jnp.where(lax.axis_index(axis) == holder, block, jnp.zeros_like(block))
    return lax.psum(block, axis)


def frequency_spectrum(filter_taps, freq_count):
    lags = jnp.arange(TAPS, dtype=jnp.float32)
    omega = 2.0 * math.pi * (FIRST_FREQUENCY + jnp.arange(freq_count, dtype=jnp.float32)) / NT
    phase = omega[:, None] * lags[None, :]
    real_part = jnp.dot(jnp.cos(phase), filter_taps, precision=lax.Precision.HIGHEST)
    imag_part = -jnp.dot(jnp.sin(phase), filter_taps, precision=lax.Precision.HIGHEST)
    return (real_part, imag_part)


def local(wavefield, panel_order, filter_taps):
    freq_count = wavefield.shape[1]
    shot_block = wavefield.shape[2]
    recv_block = wavefield.shape[3]
    own_row_index = lax.axis_index("row")
    factor = 1.0 / math.sqrt(STEPS * PANEL)
    count = 2.0 * SIDE * SIDE
    local_data = jnp.sum(jnp.square(wavefield.astype(jnp.float32)), axis=(0, 2, 3))
    energy_data = lax.psum(local_data, ("row", "col"))
    totals = jnp.zeros((freq_count, shot_block, 2 * recv_block), jnp.float32)
    for panel_advance in range(STEPS):
        first_point = panel_order[panel_advance] * PANEL
        row_width = min(PANEL, shot_block)
        owner_turn = 0
        start = first_point + owner_turn * row_width
        piece = lax.dynamic_slice_in_dim(wavefield, start % shot_block, row_width, 2)
        row_pieces = spread(piece, "row", start // shot_block)
        col_pieces = []
        mirror_width = min(shot_block, recv_block)
        for owner_turn in range(max(1, shot_block // recv_block)):
            start = own_row_index * shot_block + owner_turn * mirror_width
            piece = row_pieces
            col_pieces.append(spread(piece, "col", start // recv_block))
        upper = jnp.swapaxes(jnp.concatenate(col_pieces, axis=3), 2, 3)
        left_factor = jnp.concatenate([upper[0], upper[1]], axis=2)
        right_factor = jnp.concatenate(
            [
                jnp.concatenate([row_pieces[0], row_pieces[1]], axis=2),
                jnp.concatenate([-row_pieces[1], row_pieces[0]], axis=2),
            ],
            axis=1,
        )
        totals = totals + jnp.einsum(
            "yga,yah->ygh", left_factor, right_factor, preferred_element_type=jnp.float32
        )
    mult_re = totals[:, :, :recv_block] * factor
    mult_im = totals[:, :, recv_block:] * factor
    local_mult = jnp.sum(mult_re * mult_re, axis=(1, 2)) + jnp.sum(mult_im * mult_im, axis=(1, 2))
    energy_mult = lax.psum(local_mult, ("row", "col"))
    gain = jnp.sqrt((energy_data / count + 1e-05) / (energy_mult / count + 1e-05))[:, None, None]
    spec_re, spectrum_imaginary = frequency_spectrum(filter_taps, freq_count)
    a_re = spec_re[:, None, :]
    a_im = spectrum_imaginary[:, None, :]
    sub_re = gain * (a_re * mult_re - a_im * mult_im)
    subtracted_imaginary = gain * (a_re * mult_im + a_im * mult_re)
    result = jnp.stack(
        [
            wavefield[0].astype(jnp.float32) - sub_re,
            wavefield[1].astype(jnp.float32) - subtracted_imaginary,
        ]
    )
    return result.astype(jnp.bfloat16)


def predict_kernel(field, order, taps, plane,
                   own, right, in1, in2, left, acc, rhs, relay, energy, spec,
                   part_sums, row_sums, col_sums,
                   xs, xr, ys, yr, gs, gr, us, ds, zr, ps, pr, hs, hr, ns,
                   load_sem, rs, rr, cs, cr):
    per_panel = PANEL // CHUNK
    count = 2.0 * SIDE * SIDE
    factor = 1.0 / math.sqrt(STEPS * PANEL)
    row = lax.axis_index("row")
    col = lax.axis_index("col")
    z = col // 2
    core = col % 2
    along_x = row + 1 - 2 * (row % 2)
    along_y = (row + 2) % 4
    partner = col + 1 - 2 * core
    blocks = plane.shape[1]
    shots = blocks * CHUNK
    width = plane.shape[3]
    per_block = shots // PANEL
    above = z - row
    far = jnp.abs(above)

    quarter = blocks // 4
    loads = [
        pltpu.make_async_copy(field.at[:, pl.ds(j * quarter, quarter)],
                              plane.at[:, pl.ds(j * quarter, quarter)], load_sem.at[j])
        for j in range(4)
    ]
    for load in loads:
        load.start()
    barrier = pltpu.get_barrier_semaphore()
    for j in range(1, 4):
        pl.semaphore_signal(barrier, inc=1, device_id=((row + j) % 4, col), device_id_type=MESH)
    for j in range(1, 8):
        pl.semaphore_signal(barrier, inc=1, device_id=(row, (col + j) % 8), device_id_type=MESH)
    energy[...] = jnp.zeros_like(energy)

    re = jnp.zeros((1, width), jnp.float32)
    im = jnp.zeros((1, width), jnp.float32)
    for l in range(TAPS):
        phase = 2.0 * math.pi * FIRST_FREQUENCY / NT * l
        tap = taps[pl.ds(l, 1), :]
        re = re + math.cos(phase) * tap
        im = im - math.sin(phase) * tap
    spec[pl.ds(0, 1), :] = re
    spec[pl.ds(1, 1), :] = im
    pl.semaphore_wait(barrier, 10)

    def first_axis(k):
        return along_x + (k % 2) * (along_y - along_x)

    def second_axis(k):
        return along_y + (k % 2) * (along_x - along_y)

    def kept(k):
        return row % 2 + (k % 2) * (row // 2 - row % 2)

    def remote(src, dst, send, recv, to):
        return pltpu.make_async_remote_copy(
            src_ref=src, dst_ref=dst, send_sem=send, recv_sem=recv, device_id=to,
            device_id_type=MESH)

    def prepare(k):
        panel = order[k // per_panel]
        block = lax.rem(panel, per_block) * per_panel + k % per_panel
        mine = jnp.where(lax.div(panel, per_block) == row, 1.0, 0.0)
        for c in range(2):
            own[k, c] = (plane[c, block].astype(jnp.float32) * mine).astype(jnp.bfloat16)

    def give(k):
        return remote(own.at[k, 1 - kept(k)], in1.at[k], xs.at[0], xr.at[k], (first_axis(k), col))

    def swap(k):
        return remote(own.at[k, kept(k)], in2.at[k], ys.at[0], yr.at[k], (second_axis(k), col))

    def share(k, half):
        return remote(right.at[k, half], right.at[k, half], gs.at[0], gr.at[k],
                      (first_axis(k), col))

    def z_copy(src, k, half, to, sem):
        return remote(src, left.at[core, k, half], sem.at[0], zr.at[half, k], (row, to))

    def p_copy(src, k, half):
        return remote(src, left.at[half, k], ps.at[0], pr.at[k], (row, partner))

    def inner(k):
        return k % INNER == INNER_AT

    def outer(k, which):
        return k % OUTER == OUTER_AT[which]

    ways = []
    for way in range(2):
        at = row if way == 0 else LAST_PLANE - row
        level = z if way == 0 else LAST_PLANE - z
        to = col + 2 if way == 0 else col - 2
        ways.append((at, level, to, us if way == 0 else ds))

    def detoured(at, k):
        edge = jnp.logical_and(at == 0, jnp.logical_or(outer(k, 0), outer(k, 1)))
        return jnp.logical_or(edge, jnp.logical_and(jnp.logical_or(at == 1, at == 2), inner(k)))

    def sends(way, k):
        at, level, _, _ = ways[way]
        return jnp.logical_and(jnp.logical_and(level >= at, level < LAST_PLANE),
                               jnp.logical_not(detoured(at, k)))

    def pass_on(src, k, half):
        for way in range(2):
            @pl.when(sends(way, k))
            def _():
                z_copy(src, k, half, ways[way][2], ways[way][3]).start()

    carried = []
    for way in range(2):
        for carrier, source, to in ((1, 0, along_x), (2, 0, along_y), (3, 1, along_y), (3, 2, along_x)):
            slot = source - 1 if carrier == 3 else way
            carried.append((way, carrier, source, to, slot))

    def taken(entry, k):
        carrier = entry[1]
        return inner(k) if carrier == 3 else outer(k, carrier - 1)

    def place(entry, k):
        return k // INNER if entry[1] == 3 else k // OUTER

    def hop(entry, src, k):
        way, _, _, _, slot = entry
        n = place(entry, k)
        return remote(src, relay.at[slot, n], hs.at[slot], hr.at[slot, n], (row, ways[way][2]))

    def deliver(entry, k):
        _, _, _, to, slot = entry
        n = place(entry, k)
        return remote(relay.at[slot, n], left.at[core, k], ns.at[slot], zr.at[0, k], (to, col))

    def carrying(entry, k):
        return jnp.logical_and(ways[entry[0]][0] == entry[1],
                               jnp.logical_and(jnp.logical_and(k >= 0, k < NCHUNK), taken(entry, k)))

    def build(at, size):
        re = right[pl.ds(at, size), 0]
        im = right[pl.ds(at, size), 1]
        rhs[0, pl.ds(0, size), 0] = re
        rhs[0, pl.ds(0, size), 1] = -im
        rhs[1, pl.ds(0, size), 0] = im
        rhs[1, pl.ds(0, size), 1] = re

    def product(at, size, tile, c):
        per_half = width // TILE
        depth = 2 * size * CHUNK
        inside = pl.multiple_of((tile % per_half) * TILE, TILE)
        lhs = left[tile // per_half, pl.ds(at, size), :, :, pl.ds(inside, TILE)]
        return lax.dot_general(
            lhs.reshape(depth, TILE), rhs[c, pl.ds(0, size)].reshape(depth, width),
            (((0,), (0,)), ((), ())), preferred_element_type=jnp.float32)

    for load in loads:
        load.wait()

    @pl.loop(0, AHEAD)
    def _(k):
        prepare(k)
        give(k).start()

    @pl.loop(0, blocks)
    def _(i):
        here = pl.ds(pl.multiple_of(i * CHUNK, CHUNK), CHUNK)
        for c in range(2):
            acc[c, here, :] = jnp.zeros((CHUNK, width), jnp.float32)

    @pl.loop(0, NCHUNK + LAG)
    def _(s):
        @pl.when(s + AHEAD < NCHUNK)
        def _():
            prepare(s + AHEAD)
            give(s + AHEAD).start()

        @pl.when(s < NCHUNK)
        def _():
            give(s).wait_recv()
            own[s, kept(s)] = own[s, kept(s)] + in1[s]
            swap(s).start()

        k1 = s - HOP

        @pl.when(jnp.logical_and(k1 >= 0, k1 < NCHUNK))
        def _():
            swap(k1).wait_recv()
            right[k1, kept(k1)] = own[k1, kept(k1)] + in2[k1]
            share(k1, kept(k1)).start()

            @pl.when(above == 0)
            def _():
                pass_on(right.at[k1, kept(k1)], k1, kept(k1))
                left[core, k1, kept(k1)] = right[k1, kept(k1)]

        k2 = s - 2 * HOP

        @pl.when(jnp.logical_and(k2 >= 0, k2 < NCHUNK))
        def _():
            share(k2, 1 - kept(k2)).wait_recv()

            @pl.when(above == 0)
            def _():
                pass_on(right.at[k2, 1 - kept(k2)], k2, 1 - kept(k2))
                p_copy(right.at[k2], k2, core).start()
                left[core, k2, 1 - kept(k2)] = right[k2, 1 - kept(k2)]

        for entry in carried:
            @pl.when(jnp.logical_and(carrying(entry, k2), ways[entry[0]][1] == entry[2]))
            def _():
                hop(entry, right.at[k2], k2).start()

        toward = jnp.where(above > 0, row, LAST_PLANE - row)
        for late in range(2):
            k3 = s - HOP * (1 + late + far)

            @pl.when(jnp.logical_and(jnp.logical_and(far > 0, jnp.logical_not(detoured(toward, k3))),
                                     jnp.logical_and(k3 >= 0, k3 < NCHUNK)))
            def _():
                half = 1 - kept(k3) if late else kept(k3)
                here = left.at[core, k3, half]
                z_copy(right.at[k3, half], k3, half, partner, us).wait_recv()
                pass_on(here, k3, half)
                if late:
                    p_copy(left.at[core, k3], k3, core).start()

        for entry in carried:
            way, _, source, _, slot = entry
            level = ways[way][1]
            k4 = s - HOP * (2 + level - source)

            @pl.when(jnp.logical_and(carrying(entry, k4), level > source))
            def _():
                hop(entry, right.at[k4], k4).wait_recv()
                deliver(entry, k4).start()

                @pl.when(level < LAST_PLANE)
                def _():
                    hop(entry, relay.at[slot, place(entry, k4)], k4).start()

        k5 = s - HOP * (3 + far)

        @pl.when(jnp.logical_and(jnp.logical_and(far > 0, detoured(toward, k5)),
                                 jnp.logical_and(k5 >= 0, k5 < NCHUNK)))
        def _():
            remote(right.at[k5], left.at[core, k5], us.at[0], zr.at[0, k5], (row, partner)).wait_recv()
            p_copy(left.at[core, k5], k5, core).start()

        k6 = s - LAG

        @pl.when(jnp.logical_and(k6 >= 0, k6 < NCHUNK))
        def _():
            p_copy(right.at[k6], k6, 1 - core).wait_recv()

        @pl.when(s < blocks // STRIP)
        def _():
            for c in range(2):
                value = plane[c, pl.ds(s * STRIP, STRIP)].astype(jnp.float32)
                energy[0] = energy[0] + jnp.sum(
                    (value * value).reshape(STRIP * CHUNK // 8, 8, width), axis=0)

        step = s - (LAG + GROUP - 1)

        @pl.when(jnp.logical_and(step >= 0, step < NCHUNK - LAST))
        def _():
            part = step % GROUP
            at_chunk = step - part

            @pl.when(part == 0)
            def _():
                build(at_chunk, GROUP)

            @pl.when(part % PACE == 0)
            def _():
                tile = part // PACE
                for c in range(2):
                    here = pl.ds(pl.multiple_of(tile * TILE, TILE), TILE)
                    acc[c, here, :] = acc[c, here, :] + product(at_chunk, GROUP, tile, c)

    build(NCHUNK - LAST, LAST)

    @pl.loop(0, shots // TILE)
    def _(tile):
        for c in range(2):
            here = pl.ds(pl.multiple_of(tile * TILE, TILE), TILE)
            value = (acc[c, here, :] + product(NCHUNK - LAST, LAST, tile, c)) * factor
            acc[c, here, :] = value
            energy[1] = energy[1] + jnp.sum((value * value).reshape(TILE // 8, 8, width), axis=0)

    sums = energy[:, :, :128]
    for j in range(1, width // 128):
        sums = sums + energy[:, :, j * 128:(j + 1) * 128]
    part_sums[0] = sums
    row_copies = [
        remote(part_sums.at[0], row_sums.at[j - 1], rs.at[j - 1], rr.at[j - 1], ((row + j) % 4, col))
        for j in range(1, 4)
    ]
    for copy in row_copies:
        copy.start()

    for sem in (xs, ys, gs):
        remote(in1, in2, sem.at[0], xr.at[0], (along_x, col)).wait_send()
    remote(left.at[core], left.at[core], ps.at[0], pr.at[0], (row, partner)).wait_send()
    for way in range(2):
        at, level, _, sem = ways[way]
        for first, last, detours in ((0, 1, 2 * NCHUNK // OUTER), (1, LAST_PLANE, RELAYS)):
            part = left.at[core, pl.ds(0, NCHUNK - detours)]

            @pl.when(jnp.logical_and(jnp.logical_and(at >= first, at < last),
                                     jnp.logical_and(level >= at, level < LAST_PLANE)))
            def _():
                remote(part, part, sem.at[0], pr.at[0], (row, partner)).wait_send()
    for entry in carried:
        level = ways[entry[0]][1]
        part = relay.at[entry[4], pl.ds(0, RELAYS if entry[1] == 3 else NCHUNK // OUTER)]

        @pl.when(jnp.logical_and(ways[entry[0]][0] == entry[1], level > entry[2]))
        def _():
            remote(part, part, ns.at[entry[4]], pr.at[0], (row, partner)).wait_send()

        @pl.when(jnp.logical_and(ways[entry[0]][0] == entry[1],
                                 jnp.logical_and(level >= entry[2], level < LAST_PLANE)))
        def _():
            remote(part, part, hs.at[entry[4]], pr.at[0], (row, partner)).wait_send()

    for j in range(3):
        row_copies[j].wait_recv()
        sums = sums + row_sums[j]
    part_sums[1] = sums
    col_copies = [
        remote(part_sums.at[1], col_sums.at[j - 1], cs.at[j - 1], cr.at[j - 1], (row, (col + j) % 8))
        for j in range(1, 8)
    ]
    for copy in col_copies:
        copy.start()
    for j in range(7):
        col_copies[j].wait_recv()
        sums = sums + col_sums[j]
    data = jnp.full((1, width), jnp.sum(sums[0]), jnp.float32)
    predicted = jnp.full((1, width), jnp.sum(sums[1]), jnp.float32)
    gain = jnp.sqrt((data / count + 1e-05) / (predicted / count + 1e-05))
    re = gain * spec[pl.ds(0, 1), :]
    im = gain * spec[pl.ds(1, 1), :]

    @pl.loop(0, blocks)
    def _(j):
        for half in range(CHUNK // FINAL):
            rows = slice(half * FINAL, (half + 1) * FINAL)
            here = pl.ds(pl.multiple_of(j * CHUNK + half * FINAL, FINAL), FINAL)
            mult_re = acc[0, here, :]
            mult_im = acc[1, here, :]
            plane[0, j, rows] = (plane[0, j, rows].astype(jnp.float32)
                                  - (re * mult_re - im * mult_im)).astype(jnp.bfloat16)
            plane[1, j, rows] = (plane[1, j, rows].astype(jnp.float32)
                                  - (re * mult_im + im * mult_re)).astype(jnp.bfloat16)

    for copy in row_copies + col_copies:
        copy.wait_send()


def local_fast(wavefield, panel_order, filter_taps):
    shot_block = wavefield.shape[2]
    recv_block = wavefield.shape[3]
    block = (NCHUNK, 2, CHUNK, recv_block)
    whole = (2, shot_block // CHUNK, CHUNK, recv_block)
    dma = pltpu.SemaphoreType.DMA
    vmem = pltpu.VMEM
    result = pl.pallas_call(
        predict_kernel,
        out_shape=pltpu.VMEM(whole, jnp.bfloat16),
        in_specs=[
            pl.BlockSpec(memory_space=pl.ANY),
            pl.BlockSpec(memory_space=pltpu.SMEM),
            pl.BlockSpec(memory_space=pltpu.VMEM),
        ],
        out_specs=pl.BlockSpec(memory_space=pltpu.VMEM),
        scratch_shapes=[
            vmem(block, jnp.bfloat16),
            vmem(block, jnp.bfloat16),
            vmem((NCHUNK, CHUNK, recv_block), jnp.bfloat16),
            vmem((NCHUNK, CHUNK, recv_block), jnp.bfloat16),
            vmem((2,) + block, jnp.bfloat16),
            vmem((2, shot_block, recv_block), jnp.float32),
            vmem((2, GROUP, 2, CHUNK, recv_block), jnp.bfloat16),
            vmem((2, RELAYS, 2, CHUNK, recv_block), jnp.bfloat16),
            vmem((2, 8, recv_block), jnp.float32),
            vmem((8, recv_block), jnp.float32),
            vmem((2, 2, 8, 128), jnp.float32),
            vmem((3, 2, 8, 128), jnp.float32),
            vmem((7, 2, 8, 128), jnp.float32),
        ] + [dma((1,)), dma((NCHUNK,))] * 3 + [dma((1,)), dma((1,)), dma((2, NCHUNK))] + [
            dma((1,)), dma((NCHUNK,)), dma((2,)), dma((2, RELAYS)), dma((2,)),
            dma((4,)), dma((3,)), dma((3,)), dma((7,)), dma((7,))],
        compiler_params=pltpu.CompilerParams(
            collective_id=0, has_side_effects=True, vmem_limit_bytes=52 << 20),
        name="predict",
    )(wavefield.reshape(whole), panel_order, filter_taps)
    return result.reshape(wavefield.shape)


def solution(mesh):
    in_specs = (P(None, None, "row", "col"), P(), P(None, "col"))
    out_specs = P(None, None, "row", "col")
    fast = mesh.shape["row"] == 4 and mesh.shape["col"] == 8
    body = local_fast if fast else local
    return jax.shard_map(body, mesh=mesh, in_specs=in_specs, out_specs=out_specs, check_vma=False)
```

```python
import math

import jax
import jax.numpy as jnp
from jax import lax
from jax.experimental import pallas as pl
from jax.experimental.pallas import tpu as pltpu
from jax.sharding import PartitionSpec as P

SIDE = 8192
PANEL = 512
STEPS = 3
TAPS = 11
FIRST_FREQUENCY = 8
NT = 1024
MESH = pl.DeviceIdType.MESH

CHUNK = 32
NCHUNK = STEPS * PANEL // CHUNK
GROUP = 128 // CHUNK
TILE = 1024
LAST = GROUP
PACE = GROUP * TILE // 2048
HOP = 2
LAG = 6 * HOP + 1
AHEAD = 2
STRIP = 64 // CHUNK
FINAL = 16
INNER = 6
INNER_AT = 3
OUTER = 24
OUTER_AT = (8, 20)
RELAYS = (NCHUNK - INNER_AT + INNER - 1) // INNER
LAST_PLANE = 3


def spread(block, axis, holder):
    block = jnp.where(lax.axis_index(axis) == holder, block, jnp.zeros_like(block))
    return lax.psum(block, axis)


def frequency_spectrum(filter_taps, freq_count):
    lags = jnp.arange(TAPS, dtype=jnp.float32)
    omega = 2.0 * math.pi * (FIRST_FREQUENCY + jnp.arange(freq_count, dtype=jnp.float32)) / NT
    phase = omega[:, None] * lags[None, :]
    real_part = jnp.dot(jnp.cos(phase), filter_taps, precision=lax.Precision.HIGHEST)
    imag_part = -jnp.dot(jnp.sin(phase), filter_taps, precision=lax.Precision.HIGHEST)
    return (real_part, imag_part)


def local(wavefield, panel_order, filter_taps):
    freq_count = wavefield.shape[1]
    shot_block = wavefield.shape[2]
    recv_block = wavefield.shape[3]
    own_row_index = lax.axis_index("row")
    factor = 1.0 / math.sqrt(STEPS * PANEL)
    count = 2.0 * SIDE * SIDE
    local_data = jnp.sum(jnp.square(wavefield.astype(jnp.float32)), axis=(0, 2, 3))
    energy_data = lax.psum(local_data, ("row", "col"))
    totals = jnp.zeros((freq_count, shot_block, 2 * recv_block), jnp.float32)
    for panel_advance in range(STEPS):
        first_point = panel_order[panel_advance] * PANEL
        row_width = min(PANEL, shot_block)
        owner_turn = 0
        start = first_point + owner_turn * row_width
        piece = lax.dynamic_slice_in_dim(wavefield, start % shot_block, row_width, 2)
        row_pieces = spread(piece, "row", start // shot_block)
        col_pieces = []
        mirror_width = min(shot_block, recv_block)
        for owner_turn in range(max(1, shot_block // recv_block)):
            start = own_row_index * shot_block + owner_turn * mirror_width
            piece = row_pieces
            col_pieces.append(spread(piece, "col", start // recv_block))
        upper = jnp.swapaxes(jnp.concatenate(col_pieces, axis=3), 2, 3)
        left_factor = jnp.concatenate([upper[0], upper[1]], axis=2)
        right_factor = jnp.concatenate(
            [
                jnp.concatenate([row_pieces[0], row_pieces[1]], axis=2),
                jnp.concatenate([-row_pieces[1], row_pieces[0]], axis=2),
            ],
            axis=1,
        )
        totals = totals + jnp.einsum(
            "yga,yah->ygh", left_factor, right_factor, preferred_element_type=jnp.float32
        )
    mult_re = totals[:, :, :recv_block] * factor
    mult_im = totals[:, :, recv_block:] * factor
    local_mult = jnp.sum(mult_re * mult_re, axis=(1, 2)) + jnp.sum(mult_im * mult_im, axis=(1, 2))
    energy_mult = lax.psum(local_mult, ("row", "col"))
    gain = jnp.sqrt((energy_data / count + 1e-05) / (energy_mult / count + 1e-05))[:, None, None]
    spec_re, spectrum_imaginary = frequency_spectrum(filter_taps, freq_count)
    a_re = spec_re[:, None, :]
    a_im = spectrum_imaginary[:, None, :]
    sub_re = gain * (a_re * mult_re - a_im * mult_im)
    subtracted_imaginary = gain * (a_re * mult_im + a_im * mult_re)
    result = jnp.stack(
        [
            wavefield[0].astype(jnp.float32) - sub_re,
            wavefield[1].astype(jnp.float32) - subtracted_imaginary,
        ]
    )
    return result.astype(jnp.bfloat16)


def predict_kernel(field, order, taps, plane,
                   own, right, in1, in2, left, acc, rhs, relay, energy, spec,
                   part_sums, row_sums, col_sums,
                   xs, xr, ys, yr, gs, gr, us, ds, zr, ps, pr, hs, hr, ns,
                   load_sem, rs, rr, cs, cr):
    per_panel = PANEL // CHUNK
    count = 2.0 * SIDE * SIDE
    factor = 1.0 / math.sqrt(STEPS * PANEL)
    row = lax.axis_index("row")
    col = lax.axis_index("col")
    z = col // 2
    core = col % 2
    along_x = row + 1 - 2 * (row % 2)
    along_y = (row + 2) % 4
    partner = col + 1 - 2 * core
    blocks = plane.shape[1]
    shots = blocks * CHUNK
    width = plane.shape[3]
    per_block = shots // PANEL
    above = z - row
    far = jnp.abs(above)

    quarter = blocks // 4
    loads = [
        pltpu.make_async_copy(field.at[:, pl.ds(j * quarter, quarter)],
                              plane.at[:, pl.ds(j * quarter, quarter)], load_sem.at[j])
        for j in range(4)
    ]
    for load in loads:
        load.start()
    barrier = pltpu.get_barrier_semaphore()
    for j in range(1, 4):
        pl.semaphore_signal(barrier, inc=1, device_id=((row + j) % 4, col), device_id_type=MESH)
    for j in range(1, 8):
        pl.semaphore_signal(barrier, inc=1, device_id=(row, (col + j) % 8), device_id_type=MESH)
    energy[...] = jnp.zeros_like(energy)

    re = jnp.zeros((1, width), jnp.float32)
    im = jnp.zeros((1, width), jnp.float32)
    for l in range(TAPS):
        phase = 2.0 * math.pi * FIRST_FREQUENCY / NT * l
        tap = taps[pl.ds(l, 1), :]
        re = re + math.cos(phase) * tap
        im = im - math.sin(phase) * tap
    spec[pl.ds(0, 1), :] = re
    spec[pl.ds(1, 1), :] = im
    pl.semaphore_wait(barrier, 10)

    def first_axis(k):
        return along_x + (k % 2) * (along_y - along_x)

    def second_axis(k):
        return along_y + (k % 2) * (along_x - along_y)

    def kept(k):
        return row % 2 + (k % 2) * (row // 2 - row % 2)

    def remote(src, dst, send, recv, to):
        return pltpu.make_async_remote_copy(
            src_ref=src, dst_ref=dst, send_sem=send, recv_sem=recv, device_id=to,
            device_id_type=MESH)

    def prepare(k):
        panel = order[k // per_panel]
        block = lax.rem(panel, per_block) * per_panel + k % per_panel
        mine = jnp.where(lax.div(panel, per_block) == row, 1.0, 0.0)
        for c in range(2):
            own[k, c] = (plane[c, block].astype(jnp.float32) * mine).astype(jnp.bfloat16)

    def give(k):
        return remote(own.at[k, 1 - kept(k)], in1.at[k], xs.at[0], xr.at[k], (first_axis(k), col))

    def swap(k):
        return remote(own.at[k, kept(k)], in2.at[k], ys.at[0], yr.at[k], (second_axis(k), col))

    def share(k, half):
        return remote(right.at[k, half], right.at[k, half], gs.at[0], gr.at[k],
                      (first_axis(k), col))

    def z_copy(src, k, half, to, sem):
        return remote(src, left.at[core, k, half], sem.at[0], zr.at[half, k], (row, to))

    def p_copy(src, k, half):
        return remote(src, left.at[half, k], ps.at[0], pr.at[k], (row, partner))

    def inner(k):
        return k % INNER == INNER_AT

    def outer(k, which):
        return k % OUTER == OUTER_AT[which]

    ways = []
    for way in range(2):
        at = row if way == 0 else LAST_PLANE - row
        level = z if way == 0 else LAST_PLANE - z
        to = col + 2 if way == 0 else col - 2
        ways.append((at, level, to, us if way == 0 else ds))

    def detoured(at, k):
        edge = jnp.logical_and(at == 0, jnp.logical_or(outer(k, 0), outer(k, 1)))
        return jnp.logical_or(edge, jnp.logical_and(jnp.logical_or(at == 1, at == 2), inner(k)))

    def sends(way, k):
        at, level, _, _ = ways[way]
        return jnp.logical_and(jnp.logical_and(level >= at, level < LAST_PLANE),
                               jnp.logical_not(detoured(at, k)))

    def pass_on(src, k, half):
        for way in range(2):
            @pl.when(sends(way, k))
            def _():
                z_copy(src, k, half, ways[way][2], ways[way][3]).start()

    carried = []
    for way in range(2):
        for carrier, source, to in ((1, 0, along_x), (2, 0, along_y), (3, 1, along_y), (3, 2, along_x)):
            slot = source - 1 if carrier == 3 else way
            carried.append((way, carrier, source, to, slot))

    def taken(entry, k):
        carrier = entry[1]
        return inner(k) if carrier == 3 else outer(k, carrier - 1)

    def place(entry, k):
        return k // INNER if entry[1] == 3 else k // OUTER

    def hop(entry, src, k):
        way, _, _, _, slot = entry
        n = place(entry, k)
        return remote(src, relay.at[slot, n], hs.at[slot], hr.at[slot, n], (row, ways[way][2]))

    def deliver(entry, k):
        _, _, _, to, slot = entry
        n = place(entry, k)
        return remote(relay.at[slot, n], left.at[core, k], ns.at[slot], zr.at[0, k], (to, col))

    def carrying(entry, k):
        return jnp.logical_and(ways[entry[0]][0] == entry[1],
                               jnp.logical_and(jnp.logical_and(k >= 0, k < NCHUNK), taken(entry, k)))

    def build(at, size):
        re = right[pl.ds(at, size), 0]
        im = right[pl.ds(at, size), 1]
        rhs[0, pl.ds(0, size), 0] = re
        rhs[0, pl.ds(0, size), 1] = -im
        rhs[1, pl.ds(0, size), 0] = im
        rhs[1, pl.ds(0, size), 1] = re

    def product(at, size, tile, c):
        per_half = width // TILE
        depth = 2 * size * CHUNK
        inside = pl.multiple_of((tile % per_half) * TILE, TILE)
        lhs = left[tile // per_half, pl.ds(at, size), :, :, pl.ds(inside, TILE)]
        return lax.dot_general(
            lhs.reshape(depth, TILE), rhs[c, pl.ds(0, size)].reshape(depth, width),
            (((0,), (0,)), ((), ())), preferred_element_type=jnp.float32)

    def filter_rows(first, last):
        @pl.loop(first, last)
        def _(j):
            for half in range(CHUNK // FINAL):
                here = pl.ds(pl.multiple_of(j * CHUNK + half * FINAL, FINAL), FINAL)
                a_re = spec[pl.ds(0, 1), :]
                a_im = spec[pl.ds(1, 1), :]
                mult_re = acc[0, here, :]
                mult_im = acc[1, here, :]
                acc[0, here, :] = a_re * mult_re - a_im * mult_im
                acc[1, here, :] = a_re * mult_im + a_im * mult_re

    for load in loads:
        load.wait()

    @pl.loop(0, AHEAD)
    def _(k):
        prepare(k)
        give(k).start()

    @pl.loop(0, blocks)
    def _(i):
        here = pl.ds(pl.multiple_of(i * CHUNK, CHUNK), CHUNK)
        for c in range(2):
            acc[c, here, :] = jnp.zeros((CHUNK, width), jnp.float32)

    @pl.loop(0, NCHUNK + LAG)
    def _(s):
        @pl.when(s + AHEAD < NCHUNK)
        def _():
            prepare(s + AHEAD)
            give(s + AHEAD).start()

        @pl.when(s < NCHUNK)
        def _():
            give(s).wait_recv()
            own[s, kept(s)] = own[s, kept(s)] + in1[s]
            swap(s).start()

        k1 = s - HOP

        @pl.when(jnp.logical_and(k1 >= 0, k1 < NCHUNK))
        def _():
            swap(k1).wait_recv()
            right[k1, kept(k1)] = own[k1, kept(k1)] + in2[k1]
            share(k1, kept(k1)).start()

            @pl.when(above == 0)
            def _():
                pass_on(right.at[k1, kept(k1)], k1, kept(k1))
                left[core, k1, kept(k1)] = right[k1, kept(k1)]

        k2 = s - 2 * HOP

        @pl.when(jnp.logical_and(k2 >= 0, k2 < NCHUNK))
        def _():
            share(k2, 1 - kept(k2)).wait_recv()

            @pl.when(above == 0)
            def _():
                pass_on(right.at[k2, 1 - kept(k2)], k2, 1 - kept(k2))
                p_copy(right.at[k2], k2, core).start()
                left[core, k2, 1 - kept(k2)] = right[k2, 1 - kept(k2)]

        for entry in carried:
            @pl.when(jnp.logical_and(carrying(entry, k2), ways[entry[0]][1] == entry[2]))
            def _():
                hop(entry, right.at[k2], k2).start()

        toward = jnp.where(above > 0, row, LAST_PLANE - row)
        for late in range(2):
            k3 = s - HOP * (1 + late + far)

            @pl.when(jnp.logical_and(jnp.logical_and(far > 0, jnp.logical_not(detoured(toward, k3))),
                                     jnp.logical_and(k3 >= 0, k3 < NCHUNK)))
            def _():
                half = 1 - kept(k3) if late else kept(k3)
                here = left.at[core, k3, half]
                z_copy(right.at[k3, half], k3, half, partner, us).wait_recv()
                pass_on(here, k3, half)
                if late:
                    p_copy(left.at[core, k3], k3, core).start()

        for entry in carried:
            way, _, source, _, slot = entry
            level = ways[way][1]
            k4 = s - HOP * (2 + level - source)

            @pl.when(jnp.logical_and(carrying(entry, k4), level > source))
            def _():
                hop(entry, right.at[k4], k4).wait_recv()
                deliver(entry, k4).start()

                @pl.when(level < LAST_PLANE)
                def _():
                    hop(entry, relay.at[slot, place(entry, k4)], k4).start()

        k5 = s - HOP * (3 + far)

        @pl.when(jnp.logical_and(jnp.logical_and(far > 0, detoured(toward, k5)),
                                 jnp.logical_and(k5 >= 0, k5 < NCHUNK)))
        def _():
            remote(right.at[k5], left.at[core, k5], us.at[0], zr.at[0, k5], (row, partner)).wait_recv()
            p_copy(left.at[core, k5], k5, core).start()

        k6 = s - LAG

        @pl.when(jnp.logical_and(k6 >= 0, k6 < NCHUNK))
        def _():
            p_copy(right.at[k6], k6, 1 - core).wait_recv()

        @pl.when(s < blocks // STRIP)
        def _():
            for c in range(2):
                value = plane[c, pl.ds(s * STRIP, STRIP)].astype(jnp.float32)
                energy[0] = energy[0] + jnp.sum(
                    (value * value).reshape(STRIP * CHUNK // 8, 8, width), axis=0)

        step = s - (LAG + GROUP - 1)

        @pl.when(jnp.logical_and(step >= 0, step < NCHUNK - LAST))
        def _():
            part = step % GROUP
            at_chunk = step - part

            @pl.when(part == 0)
            def _():
                build(at_chunk, GROUP)

            @pl.when(part % PACE == 0)
            def _():
                tile = part // PACE
                for c in range(2):
                    here = pl.ds(pl.multiple_of(tile * TILE, TILE), TILE)
                    acc[c, here, :] = acc[c, here, :] + product(at_chunk, GROUP, tile, c)

    build(NCHUNK - LAST, LAST)

    @pl.loop(0, shots // TILE)
    def _(tile):
        for c in range(2):
            here = pl.ds(pl.multiple_of(tile * TILE, TILE), TILE)
            value = (acc[c, here, :] + product(NCHUNK - LAST, LAST, tile, c)) * factor
            acc[c, here, :] = value
            energy[1] = energy[1] + jnp.sum((value * value).reshape(TILE // 8, 8, width), axis=0)

    sums = energy[:, :, :128]
    for j in range(1, width // 128):
        sums = sums + energy[:, :, j * 128:(j + 1) * 128]
    part_sums[0] = sums
    row_copies = [
        remote(part_sums.at[0], row_sums.at[j - 1], rs.at[j - 1], rr.at[j - 1], ((row + j) % 4, col))
        for j in range(1, 4)
    ]
    for copy in row_copies:
        copy.start()

    for sem in (xs, ys, gs):
        remote(in1, in2, sem.at[0], xr.at[0], (along_x, col)).wait_send()
    remote(left.at[core], left.at[core], ps.at[0], pr.at[0], (row, partner)).wait_send()
    for way in range(2):
        at, level, _, sem = ways[way]
        for first, last, detours in ((0, 1, 2 * NCHUNK // OUTER), (1, LAST_PLANE, RELAYS)):
            part = left.at[core, pl.ds(0, NCHUNK - detours)]

            @pl.when(jnp.logical_and(jnp.logical_and(at >= first, at < last),
                                     jnp.logical_and(level >= at, level < LAST_PLANE)))
            def _():
                remote(part, part, sem.at[0], pr.at[0], (row, partner)).wait_send()
    for entry in carried:
        level = ways[entry[0]][1]
        part = relay.at[entry[4], pl.ds(0, RELAYS if entry[1] == 3 else NCHUNK // OUTER)]

        @pl.when(jnp.logical_and(ways[entry[0]][0] == entry[1], level > entry[2]))
        def _():
            remote(part, part, ns.at[entry[4]], pr.at[0], (row, partner)).wait_send()

        @pl.when(jnp.logical_and(ways[entry[0]][0] == entry[1],
                                 jnp.logical_and(level >= entry[2], level < LAST_PLANE)))
        def _():
            remote(part, part, hs.at[entry[4]], pr.at[0], (row, partner)).wait_send()

    filter_rows(0, blocks // 2)
    for j in range(3):
        row_copies[j].wait_recv()
        sums = sums + row_sums[j]
    part_sums[1] = sums
    col_copies = [
        remote(part_sums.at[1], col_sums.at[j - 1], cs.at[j - 1], cr.at[j - 1], (row, (col + j) % 8))
        for j in range(1, 8)
    ]
    for copy in col_copies:
        copy.start()
    filter_rows(blocks // 2, blocks)
    for j in range(7):
        col_copies[j].wait_recv()
        sums = sums + col_sums[j]
    data = jnp.full((1, width), jnp.sum(sums[0]), jnp.float32)
    predicted = jnp.full((1, width), jnp.sum(sums[1]), jnp.float32)
    gain = jnp.sqrt((data / count + 1e-05) / (predicted / count + 1e-05))

    @pl.loop(0, blocks)
    def _(j):
        for half in range(CHUNK // FINAL):
            rows = slice(half * FINAL, (half + 1) * FINAL)
            here = pl.ds(pl.multiple_of(j * CHUNK + half * FINAL, FINAL), FINAL)
            for c in range(2):
                plane[c, j, rows] = (plane[c, j, rows].astype(jnp.float32)
                                     - gain * acc[c, here, :]).astype(jnp.bfloat16)

    for copy in row_copies + col_copies:
        copy.wait_send()


def local_fast(wavefield, panel_order, filter_taps):
    shot_block = wavefield.shape[2]
    recv_block = wavefield.shape[3]
    block = (NCHUNK, 2, CHUNK, recv_block)
    whole = (2, shot_block // CHUNK, CHUNK, recv_block)
    dma = pltpu.SemaphoreType.DMA
    vmem = pltpu.VMEM
    result = pl.pallas_call(
        predict_kernel,
        out_shape=pltpu.VMEM(whole, jnp.bfloat16),
        in_specs=[
            pl.BlockSpec(memory_space=pl.ANY),
            pl.BlockSpec(memory_space=pltpu.SMEM),
            pl.BlockSpec(memory_space=pltpu.VMEM),
        ],
        out_specs=pl.BlockSpec(memory_space=pltpu.VMEM),
        scratch_shapes=[
            vmem(block, jnp.bfloat16),
            vmem(block, jnp.bfloat16),
            vmem((NCHUNK, CHUNK, recv_block), jnp.bfloat16),
            vmem((NCHUNK, CHUNK, recv_block), jnp.bfloat16),
            vmem((2,) + block, jnp.bfloat16),
            vmem((2, shot_block, recv_block), jnp.float32),
            vmem((2, GROUP, 2, CHUNK, recv_block), jnp.bfloat16),
            vmem((2, RELAYS, 2, CHUNK, recv_block), jnp.bfloat16),
            vmem((2, 8, recv_block), jnp.float32),
            vmem((8, recv_block), jnp.float32),
            vmem((2, 2, 8, 128), jnp.float32),
            vmem((3, 2, 8, 128), jnp.float32),
            vmem((7, 2, 8, 128), jnp.float32),
        ] + [dma((1,)), dma((NCHUNK,))] * 3 + [dma((1,)), dma((1,)), dma((2, NCHUNK))] + [
            dma((1,)), dma((NCHUNK,)), dma((2,)), dma((2, RELAYS)), dma((2,)),
            dma((4,)), dma((3,)), dma((3,)), dma((7,)), dma((7,))],
        compiler_params=pltpu.CompilerParams(
            collective_id=0, has_side_effects=True, vmem_limit_bytes=55 << 20),
        name="predict",
    )(wavefield.reshape(whole), panel_order, filter_taps)
    return result.reshape(wavefield.shape)


def solution(mesh):
    in_specs = (P(None, None, "row", "col"), P(), P(None, "col"))
    out_specs = P(None, None, "row", "col")
    fast = mesh.shape["row"] == 4 and mesh.shape["col"] == 8
    body = local_fast if fast else local
    return jax.shard_map(body, mesh=mesh, in_specs=in_specs, out_specs=out_specs, check_vma=False)
```

```python
import math

import jax
import jax.numpy as jnp
from jax import lax
from jax.experimental import pallas as pl
from jax.experimental.pallas import tpu as pltpu
from jax.sharding import PartitionSpec as P

SIDE = 8192
PANEL = 512
STEPS = 3
TAPS = 11
FIRST_FREQUENCY = 8
NT = 1024
MESH = pl.DeviceIdType.MESH

CHUNK = 32
NCHUNK = STEPS * PANEL // CHUNK
GROUP = 128 // CHUNK
TILE = 1024
LAST = GROUP
PACE = GROUP * TILE // 2048
HOP = 2
LAG = 6 * HOP + 1
AHEAD = 2
STRIP = 64 // CHUNK
FINAL = 16
INNER = 6
INNER_AT = 3
OUTER = 24
OUTER_AT = (8, 20)
RELAYS = (NCHUNK - INNER_AT + INNER - 1) // INNER
LAST_PLANE = 3


def spread(block, axis, holder):
    block = jnp.where(lax.axis_index(axis) == holder, block, jnp.zeros_like(block))
    return lax.psum(block, axis)


def frequency_spectrum(filter_taps, freq_count):
    lags = jnp.arange(TAPS, dtype=jnp.float32)
    omega = 2.0 * math.pi * (FIRST_FREQUENCY + jnp.arange(freq_count, dtype=jnp.float32)) / NT
    phase = omega[:, None] * lags[None, :]
    real_part = jnp.dot(jnp.cos(phase), filter_taps, precision=lax.Precision.HIGHEST)
    imag_part = -jnp.dot(jnp.sin(phase), filter_taps, precision=lax.Precision.HIGHEST)
    return (real_part, imag_part)


def local(wavefield, panel_order, filter_taps):
    freq_count = wavefield.shape[1]
    shot_block = wavefield.shape[2]
    recv_block = wavefield.shape[3]
    own_row_index = lax.axis_index("row")
    factor = 1.0 / math.sqrt(STEPS * PANEL)
    count = 2.0 * SIDE * SIDE
    local_data = jnp.sum(jnp.square(wavefield.astype(jnp.float32)), axis=(0, 2, 3))
    energy_data = lax.psum(local_data, ("row", "col"))
    totals = jnp.zeros((freq_count, shot_block, 2 * recv_block), jnp.float32)
    for panel_advance in range(STEPS):
        first_point = panel_order[panel_advance] * PANEL
        row_width = min(PANEL, shot_block)
        owner_turn = 0
        start = first_point + owner_turn * row_width
        piece = lax.dynamic_slice_in_dim(wavefield, start % shot_block, row_width, 2)
        row_pieces = spread(piece, "row", start // shot_block)
        col_pieces = []
        mirror_width = min(shot_block, recv_block)
        for owner_turn in range(max(1, shot_block // recv_block)):
            start = own_row_index * shot_block + owner_turn * mirror_width
            piece = row_pieces
            col_pieces.append(spread(piece, "col", start // recv_block))
        upper = jnp.swapaxes(jnp.concatenate(col_pieces, axis=3), 2, 3)
        left_factor = jnp.concatenate([upper[0], upper[1]], axis=2)
        right_factor = jnp.concatenate(
            [
                jnp.concatenate([row_pieces[0], row_pieces[1]], axis=2),
                jnp.concatenate([-row_pieces[1], row_pieces[0]], axis=2),
            ],
            axis=1,
        )
        totals = totals + jnp.einsum(
            "yga,yah->ygh", left_factor, right_factor, preferred_element_type=jnp.float32
        )
    mult_re = totals[:, :, :recv_block] * factor
    mult_im = totals[:, :, recv_block:] * factor
    local_mult = jnp.sum(mult_re * mult_re, axis=(1, 2)) + jnp.sum(mult_im * mult_im, axis=(1, 2))
    energy_mult = lax.psum(local_mult, ("row", "col"))
    gain = jnp.sqrt((energy_data / count + 1e-05) / (energy_mult / count + 1e-05))[:, None, None]
    spec_re, spectrum_imaginary = frequency_spectrum(filter_taps, freq_count)
    a_re = spec_re[:, None, :]
    a_im = spectrum_imaginary[:, None, :]
    sub_re = gain * (a_re * mult_re - a_im * mult_im)
    subtracted_imaginary = gain * (a_re * mult_im + a_im * mult_re)
    result = jnp.stack(
        [
            wavefield[0].astype(jnp.float32) - sub_re,
            wavefield[1].astype(jnp.float32) - subtracted_imaginary,
        ]
    )
    return result.astype(jnp.bfloat16)


def predict_kernel(field, order, taps, plane,
                   own, right, in1, in2, left, acc, rhs, relay, energy, spec,
                   part_sums, row_sums, col_sums,
                   xs, xr, ys, yr, gs, gr, us, ds, zr, ps, pr, hs, hr, ns,
                   load_sem, rs, rr, cs, cr):
    per_panel = PANEL // CHUNK
    count = 2.0 * SIDE * SIDE
    factor = 1.0 / math.sqrt(STEPS * PANEL)
    row = lax.axis_index("row")
    col = lax.axis_index("col")
    z = col // 2
    core = col % 2
    along_x = row + 1 - 2 * (row % 2)
    along_y = (row + 2) % 4
    partner = col + 1 - 2 * core
    blocks = plane.shape[1]
    shots = blocks * CHUNK
    width = plane.shape[3]
    per_block = shots // PANEL
    above = z - row
    far = jnp.abs(above)

    quarter = blocks // 4
    loads = [
        pltpu.make_async_copy(field.at[:, pl.ds(j * quarter, quarter)],
                              plane.at[:, pl.ds(j * quarter, quarter)], load_sem.at[j])
        for j in range(4)
    ]
    for load in loads:
        load.start()
    barrier = pltpu.get_barrier_semaphore()
    for j in range(1, 4):
        pl.semaphore_signal(barrier, inc=1, device_id=((row + j) % 4, col), device_id_type=MESH)
    for j in range(1, 8):
        pl.semaphore_signal(barrier, inc=1, device_id=(row, (col + j) % 8), device_id_type=MESH)
    energy[...] = jnp.zeros_like(energy)

    re = jnp.zeros((1, width), jnp.float32)
    im = jnp.zeros((1, width), jnp.float32)
    for l in range(TAPS):
        phase = 2.0 * math.pi * FIRST_FREQUENCY / NT * l
        tap = taps[pl.ds(l, 1), :]
        re = re + math.cos(phase) * tap
        im = im - math.sin(phase) * tap
    spec[pl.ds(0, 1), :] = re
    spec[pl.ds(1, 1), :] = im
    pl.semaphore_wait(barrier, 10)

    def first_axis(k):
        return along_x + (k % 2) * (along_y - along_x)

    def second_axis(k):
        return along_y + (k % 2) * (along_x - along_y)

    def kept(k):
        return row % 2 + (k % 2) * (row // 2 - row % 2)

    def remote(src, dst, send, recv, to):
        return pltpu.make_async_remote_copy(
            src_ref=src, dst_ref=dst, send_sem=send, recv_sem=recv, device_id=to,
            device_id_type=MESH)

    def prepare(k):
        panel = order[k // per_panel]
        block = lax.rem(panel, per_block) * per_panel + k % per_panel
        mine = jnp.where(lax.div(panel, per_block) == row, 1.0, 0.0)
        for c in range(2):
            own[k, c] = (plane[c, block].astype(jnp.float32) * mine).astype(jnp.bfloat16)

    def give(k):
        return remote(own.at[k, 1 - kept(k)], in1.at[k], xs.at[0], xr.at[k], (first_axis(k), col))

    def swap(k):
        return remote(own.at[k, kept(k)], in2.at[k], ys.at[0], yr.at[k], (second_axis(k), col))

    def share(k, half):
        return remote(right.at[k, half], right.at[k, half], gs.at[0], gr.at[k],
                      (first_axis(k), col))

    def z_copy(src, k, half, to, sem):
        return remote(src, left.at[core, k, half], sem.at[0], zr.at[half, k], (row, to))

    def p_copy(src, k, half):
        return remote(src, left.at[half, k], ps.at[0], pr.at[k], (row, partner))

    def inner(k):
        return k % INNER == INNER_AT

    def outer(k, which):
        return k % OUTER == OUTER_AT[which]

    ways = []
    for way in range(2):
        at = row if way == 0 else LAST_PLANE - row
        level = z if way == 0 else LAST_PLANE - z
        to = col + 2 if way == 0 else col - 2
        ways.append((at, level, to, us if way == 0 else ds))

    def detoured(at, k):
        edge = jnp.logical_and(at == 0, jnp.logical_or(outer(k, 0), outer(k, 1)))
        return jnp.logical_or(edge, jnp.logical_and(jnp.logical_or(at == 1, at == 2), inner(k)))

    def sends(way, k):
        at, level, _, _ = ways[way]
        return jnp.logical_and(jnp.logical_and(level >= at, level < LAST_PLANE),
                               jnp.logical_not(detoured(at, k)))

    def pass_on(src, k, half):
        for way in range(2):
            @pl.when(sends(way, k))
            def _():
                z_copy(src, k, half, ways[way][2], ways[way][3]).start()

    carried = []
    for way in range(2):
        for carrier, source, to in ((1, 0, along_x), (2, 0, along_y), (3, 1, along_y), (3, 2, along_x)):
            slot = source - 1 if carrier == 3 else way
            carried.append((way, carrier, source, to, slot))

    def taken(entry, k):
        carrier = entry[1]
        return inner(k) if carrier == 3 else outer(k, carrier - 1)

    def place(entry, k):
        return k // INNER if entry[1] == 3 else k // OUTER

    def hop(entry, src, k):
        way, _, _, _, slot = entry
        n = place(entry, k)
        return remote(src, relay.at[slot, n], hs.at[slot], hr.at[slot, n], (row, ways[way][2]))

    def deliver(entry, k):
        _, _, _, to, slot = entry
        n = place(entry, k)
        return remote(relay.at[slot, n], left.at[core, k], ns.at[slot], zr.at[0, k], (to, col))

    def carrying(entry, k):
        return jnp.logical_and(ways[entry[0]][0] == entry[1],
                               jnp.logical_and(jnp.logical_and(k >= 0, k < NCHUNK), taken(entry, k)))

    def build(at, size):
        re = right[pl.ds(at, size), 0]
        im = right[pl.ds(at, size), 1]
        rhs[0, pl.ds(0, size), 0] = re
        rhs[0, pl.ds(0, size), 1] = -im
        rhs[1, pl.ds(0, size), 0] = im
        rhs[1, pl.ds(0, size), 1] = re

    def product(at, size, tile, c):
        per_half = width // TILE
        depth = 2 * size * CHUNK
        inside = pl.multiple_of((tile % per_half) * TILE, TILE)
        lhs = left[tile // per_half, pl.ds(at, size), :, :, pl.ds(inside, TILE)]
        return lax.dot_general(
            lhs.reshape(depth, TILE), rhs[c, pl.ds(0, size)].reshape(depth, width),
            (((0,), (0,)), ((), ())), preferred_element_type=jnp.float32)

    def filter_rows(first, last):
        @pl.loop(first, last)
        def _(j):
            for half in range(CHUNK // FINAL):
                here = pl.ds(pl.multiple_of(j * CHUNK + half * FINAL, FINAL), FINAL)
                a_re = spec[pl.ds(0, 1), :]
                a_im = spec[pl.ds(1, 1), :]
                mult_re = acc[0, here, :]
                mult_im = acc[1, here, :]
                acc[0, here, :] = a_re * mult_re - a_im * mult_im
                acc[1, here, :] = a_re * mult_im + a_im * mult_re

    for load in loads:
        load.wait()

    @pl.loop(0, AHEAD)
    def _(k):
        prepare(k)
        give(k).start()

    @pl.loop(0, blocks)
    def _(i):
        here = pl.ds(pl.multiple_of(i * CHUNK, CHUNK), CHUNK)
        for c in range(2):
            acc[c, here, :] = jnp.zeros((CHUNK, width), jnp.float32)

    @pl.loop(0, NCHUNK + LAG)
    def _(s):
        @pl.when(s + AHEAD < NCHUNK)
        def _():
            prepare(s + AHEAD)
            give(s + AHEAD).start()

        @pl.when(s < NCHUNK)
        def _():
            give(s).wait_recv()
            own[s, kept(s)] = own[s, kept(s)] + in1[s]
            swap(s).start()

        k1 = s - HOP

        @pl.when(jnp.logical_and(k1 >= 0, k1 < NCHUNK))
        def _():
            swap(k1).wait_recv()
            right[k1, kept(k1)] = own[k1, kept(k1)] + in2[k1]
            share(k1, kept(k1)).start()

            @pl.when(above == 0)
            def _():
                pass_on(right.at[k1, kept(k1)], k1, kept(k1))
                left[core, k1, kept(k1)] = right[k1, kept(k1)]

        k2 = s - 2 * HOP

        @pl.when(jnp.logical_and(k2 >= 0, k2 < NCHUNK))
        def _():
            share(k2, 1 - kept(k2)).wait_recv()

            @pl.when(above == 0)
            def _():
                pass_on(right.at[k2, 1 - kept(k2)], k2, 1 - kept(k2))
                p_copy(right.at[k2], k2, core).start()
                left[core, k2, 1 - kept(k2)] = right[k2, 1 - kept(k2)]

        for entry in carried:
            @pl.when(jnp.logical_and(carrying(entry, k2), ways[entry[0]][1] == entry[2]))
            def _():
                hop(entry, right.at[k2], k2).start()

        toward = jnp.where(above > 0, row, LAST_PLANE - row)
        for late in range(2):
            k3 = s - HOP * (1 + late + far)

            @pl.when(jnp.logical_and(jnp.logical_and(far > 0, jnp.logical_not(detoured(toward, k3))),
                                     jnp.logical_and(k3 >= 0, k3 < NCHUNK)))
            def _():
                half = 1 - kept(k3) if late else kept(k3)
                here = left.at[core, k3, half]
                z_copy(right.at[k3, half], k3, half, partner, us).wait_recv()
                pass_on(here, k3, half)
                if late:
                    p_copy(left.at[core, k3], k3, core).start()

        for entry in carried:
            way, _, source, _, slot = entry
            level = ways[way][1]
            k4 = s - HOP * (2 + level - source)

            @pl.when(jnp.logical_and(carrying(entry, k4), level > source))
            def _():
                hop(entry, right.at[k4], k4).wait_recv()
                deliver(entry, k4).start()

                @pl.when(level < LAST_PLANE)
                def _():
                    hop(entry, relay.at[slot, place(entry, k4)], k4).start()

        k5 = s - HOP * (3 + far)

        @pl.when(jnp.logical_and(jnp.logical_and(far > 0, detoured(toward, k5)),
                                 jnp.logical_and(k5 >= 0, k5 < NCHUNK)))
        def _():
            remote(right.at[k5], left.at[core, k5], us.at[0], zr.at[0, k5], (row, partner)).wait_recv()
            p_copy(left.at[core, k5], k5, core).start()

        k6 = s - LAG

        @pl.when(jnp.logical_and(k6 >= 0, k6 < NCHUNK))
        def _():
            p_copy(right.at[k6], k6, 1 - core).wait_recv()

        @pl.when(s < blocks // STRIP)
        def _():
            for c in range(2):
                value = plane[c, pl.ds(s * STRIP, STRIP)].astype(jnp.float32)
                energy[0] = energy[0] + jnp.sum(
                    (value * value).reshape(STRIP * CHUNK // 8, 8, width), axis=0)

        step = s - (LAG + GROUP - 1)

        @pl.when(jnp.logical_and(step >= 0, step < NCHUNK - LAST))
        def _():
            part = step % GROUP
            at_chunk = step - part

            @pl.when(part == 0)
            def _():
                build(at_chunk, GROUP)

            @pl.when(part % PACE == 0)
            def _():
                tile = part // PACE
                for c in range(2):
                    here = pl.ds(pl.multiple_of(tile * TILE, TILE), TILE)
                    acc[c, here, :] = acc[c, here, :] + product(at_chunk, GROUP, tile, c)

    build(NCHUNK - LAST, LAST)

    @pl.loop(0, shots // TILE)
    def _(tile):
        for c in range(2):
            here = pl.ds(pl.multiple_of(tile * TILE, TILE), TILE)
            value = (acc[c, here, :] + product(NCHUNK - LAST, LAST, tile, c)) * factor
            acc[c, here, :] = value
            energy[1] = energy[1] + jnp.sum((value * value).reshape(TILE // 8, 8, width), axis=0)

    sums = energy[:, :, :128]
    for j in range(1, width // 128):
        sums = sums + energy[:, :, j * 128:(j + 1) * 128]
    part_sums[0] = sums
    row_copies = [
        remote(part_sums.at[0], row_sums.at[j - 1], rs.at[j - 1], rr.at[j - 1], ((row + j) % 4, col))
        for j in range(1, 4)
    ]
    for copy in row_copies:
        copy.start()

    for sem in (xs, ys, gs):
        remote(in1, in2, sem.at[0], xr.at[0], (along_x, col)).wait_send()
    remote(left.at[core], left.at[core], ps.at[0], pr.at[0], (row, partner)).wait_send()
    for way in range(2):
        at, level, _, sem = ways[way]
        for first, last, detours in ((0, 1, 2 * NCHUNK // OUTER), (1, LAST_PLANE, RELAYS)):
            part = left.at[core, pl.ds(0, NCHUNK - detours)]

            @pl.when(jnp.logical_and(jnp.logical_and(at >= first, at < last),
                                     jnp.logical_and(level >= at, level < LAST_PLANE)))
            def _():
                remote(part, part, sem.at[0], pr.at[0], (row, partner)).wait_send()
    for entry in carried:
        level = ways[entry[0]][1]
        part = relay.at[entry[4], pl.ds(0, RELAYS if entry[1] == 3 else NCHUNK // OUTER)]

        @pl.when(jnp.logical_and(ways[entry[0]][0] == entry[1], level > entry[2]))
        def _():
            remote(part, part, ns.at[entry[4]], pr.at[0], (row, partner)).wait_send()

        @pl.when(jnp.logical_and(ways[entry[0]][0] == entry[1],
                                 jnp.logical_and(level >= entry[2], level < LAST_PLANE)))
        def _():
            remote(part, part, hs.at[entry[4]], pr.at[0], (row, partner)).wait_send()

    filter_rows(0, 3 * blocks // 8)
    for j in range(3):
        row_copies[j].wait_recv()
        sums = sums + row_sums[j]
    part_sums[1] = sums
    col_copies = [
        remote(part_sums.at[1], col_sums.at[j - 1], cs.at[j - 1], cr.at[j - 1], (row, (col + j) % 8))
        for j in range(1, 8)
    ]
    for copy in col_copies:
        copy.start()
    filter_rows(3 * blocks // 8, blocks)
    for j in range(7):
        col_copies[j].wait_recv()
        sums = sums + col_sums[j]
    data = jnp.full((1, width), jnp.sum(sums[0]), jnp.float32)
    predicted = jnp.full((1, width), jnp.sum(sums[1]), jnp.float32)
    gain = jnp.sqrt((data / count + 1e-05) / (predicted / count + 1e-05))

    @pl.loop(0, blocks)
    def _(j):
        for half in range(CHUNK // FINAL):
            rows = slice(half * FINAL, (half + 1) * FINAL)
            here = pl.ds(pl.multiple_of(j * CHUNK + half * FINAL, FINAL), FINAL)
            for c in range(2):
                plane[c, j, rows] = (plane[c, j, rows].astype(jnp.float32)
                                     - gain * acc[c, here, :]).astype(jnp.bfloat16)

    for copy in row_copies + col_copies:
        copy.wait_send()


def local_fast(wavefield, panel_order, filter_taps):
    shot_block = wavefield.shape[2]
    recv_block = wavefield.shape[3]
    block = (NCHUNK, 2, CHUNK, recv_block)
    whole = (2, shot_block // CHUNK, CHUNK, recv_block)
    dma = pltpu.SemaphoreType.DMA
    vmem = pltpu.VMEM
    result = pl.pallas_call(
        predict_kernel,
        out_shape=pltpu.VMEM(whole, jnp.bfloat16),
        in_specs=[
            pl.BlockSpec(memory_space=pl.ANY),
            pl.BlockSpec(memory_space=pltpu.SMEM),
            pl.BlockSpec(memory_space=pltpu.VMEM),
        ],
        out_specs=pl.BlockSpec(memory_space=pltpu.VMEM),
        scratch_shapes=[
            vmem(block, jnp.bfloat16),
            vmem(block, jnp.bfloat16),
            vmem((NCHUNK, CHUNK, recv_block), jnp.bfloat16),
            vmem((NCHUNK, CHUNK, recv_block), jnp.bfloat16),
            vmem((2,) + block, jnp.bfloat16),
            vmem((2, shot_block, recv_block), jnp.float32),
            vmem((2, GROUP, 2, CHUNK, recv_block), jnp.bfloat16),
            vmem((2, RELAYS, 2, CHUNK, recv_block), jnp.bfloat16),
            vmem((2, 8, recv_block), jnp.float32),
            vmem((8, recv_block), jnp.float32),
            vmem((2, 2, 8, 128), jnp.float32),
            vmem((3, 2, 8, 128), jnp.float32),
            vmem((7, 2, 8, 128), jnp.float32),
        ] + [dma((1,)), dma((NCHUNK,))] * 3 + [dma((1,)), dma((1,)), dma((2, NCHUNK))] + [
            dma((1,)), dma((NCHUNK,)), dma((2,)), dma((2, RELAYS)), dma((2,)),
            dma((4,)), dma((3,)), dma((3,)), dma((7,)), dma((7,))],
        compiler_params=pltpu.CompilerParams(
            collective_id=0, has_side_effects=True, vmem_limit_bytes=55 << 20),
        name="predict",
    )(wavefield.reshape(whole), panel_order, filter_taps)
    return result.reshape(wavefield.shape)


def solution(mesh):
    in_specs = (P(None, None, "row", "col"), P(), P(None, "col"))
    out_specs = P(None, None, "row", "col")
    fast = mesh.shape["row"] == 4 and mesh.shape["col"] == 8
    body = local_fast if fast else local
    return jax.shard_map(body, mesh=mesh, in_specs=in_specs, out_specs=out_specs, check_vma=False)
```
